32 devices in a mesh: groups: 2 (over y), seq: 4 (over z), dp: 2 (over x), sub: 2 (over core).
Axes of the slice: x: 2, y: 2, z: 4, core: 2. Of those that a mesh axis runs over, the one named last changes fastest.
Arguments:
- queries: bfloat16 [4, 512, 2048], P(('groups', 'dp'), 'seq', 'sub'), parts along dimension 0, may hold values from 0.019897461 to 1
- key_vectors: bfloat16 [4, 512, 2048], P(('groups', 'dp'), 'seq', 'sub'), parts along dimension 0, may hold values from 0.019897461 to 1
- value_vectors: bfloat16 [4, 512, 2048], P(('groups', 'dp'), 'seq', 'sub'), parts along dimension 0, may hold values from -6 to 6
- out_weight: bfloat16 [2048, 4096], P('sub', ('seq', 'dp')), may hold values from -0.125 to 0.125
- out_cotangent: bfloat16 [4, 512, 4096], P(('groups', 'dp'), 'seq'), parts along dimension 0, may hold values from -6 to 6
Outputs:
- layer_output: bfloat16 [4, 512, 4096], P(('groups', 'dp'), 'seq', 'sub'), parts along dimension 0
- query_grad: bfloat16 [4, 512, 2048], P(('groups', 'dp'), 'seq', 'sub'), parts along dimension 0
- key_grad: bfloat16 [4, 512, 2048], P(('groups', 'dp'), 'seq', 'sub'), parts along dimension 0
- value_grad: bfloat16 [4, 512, 2048], P(('groups', 'dp'), 'seq', 'sub'), parts along dimension 0
The draws below stay inside these ranges and needn't reach their ends.
There are 2 independent parts, one for each index of `groups`. The reference program is written for one: setup_inputs(seed, part) draws one part's arguments, and reference() takes and returns one part's arrays. A program takes and returns all parts, laid end to end along the dimension named above; an argument that names none is the same for every part. Nothing has to cross between parts.
All inputs are finite; a program needn't handle non-finite values.
Results may differ from the reference program's by a relative error of at most 0.009.
Values may be sent and summed in bfloat16 or wider, within the bound.
A program may use at most 128 MiB of HBM per device.

```python
import math
import jax
import jax.numpy as jnp
from jax import lax

D = 4096
HEADS = 16
HS = 128
CH = 128
SEQS = 2
LEN = 512


def steps_of(key, shape, cuts, smallest, high):
    loudness, own = 1.0, jax.random.fold_in(key, 6)
    for axis_at, shards_of in cuts:
        steps = jnp.exp(jax.random.uniform(jax.random.fold_in(own, axis_at), (shards_of,), jnp.float32, smallest / len(cuts), high / len(cuts)))
        loudness = loudness * jnp.repeat(steps, shape[axis_at] // shards_of).reshape([-1 if axis == axis_at else 1 for axis in range(len(shape))])
    return loudness


def normal_values(rng, dims, width, most, pieces=(), kind=jnp.bfloat16):
    values = jax.random.normal(rng, dims, jnp.float32) * width
    if len(pieces) > 0:
        values = steps_of(rng, dims, pieces, -0.22, 0.18) * values
    return jnp.clip(values, min=-most, max=most).astype(kind)


def setup_inputs(seed: int = 0, part: int = 0) -> dict:
    keys = jax.random.split(jax.random.key(seed), 6)
    own_keys = jax.random.split(jax.random.fold_in(keys[5], part), 6)
    queries = jnp.clip(jnp.exp(math.log(1.0) - 3.9171631 * jax.random.uniform(own_keys[0], (SEQS, LEN, HEADS * HS), jnp.float32) ** steps_of(own_keys[0], (SEQS, LEN, HEADS * HS), ((0, 2), (1, 4), (2, 2)), -0.2, 0.2)), 0.019897461, 1.0).astype(jnp.bfloat16)
    key_vectors = jnp.clip(jnp.exp(math.log(1.0) - 3.9171631 * jax.random.uniform(own_keys[1], (SEQS, LEN, HEADS * HS), jnp.float32) ** steps_of(own_keys[1], (SEQS, LEN, HEADS * HS), ((0, 2), (1, 4), (2, 2)), -0.2, 0.2)), 0.019897461, 1.0).astype(jnp.bfloat16)
    value_vectors = normal_values(own_keys[2], (SEQS, LEN, HEADS * HS), 1.0, 6.0, ((0, 2), (1, 4), (2, 2)))
    out_weight = normal_values(keys[3], (HEADS * HS, D), (HEADS * HS) ** -0.5, 0.125, ((0, 2), (1, 8)))
    out_cotangent = normal_values(own_keys[4], (SEQS, LEN, D), 1.0, 6.0, ((0, 2), (1, 4)))
    return {"queries": queries, "key_vectors": key_vectors, "value_vectors": value_vectors, "out_weight": out_weight, "out_cotangent": out_cotangent}


def rounded(tensor):
    return lax.optimization_barrier(tensor.astype(jnp.bfloat16)).astype(jnp.float32)

def rms_factor(attention):
    return lax.rsqrt(lax.optimization_barrier(jnp.mean(attention * attention, axis=-1, keepdims=True)) + 1e-05)

def reference(queries, key_vectors, value_vectors, out_weight, out_cotangent):
    sequences, length, features = queries.shape
    blocks = length // CH

    def to_heads(tensor):
        return tensor.astype(jnp.float32).reshape(sequences, blocks, CH, HEADS, HS)
    query_heads = to_heads(queries)
    key_heads = to_heads(key_vectors)
    value_heads = to_heads(value_vectors)
    positions = lax.broadcasted_iota(jnp.int32, (CH, CH), 0)
    columns = lax.broadcasted_iota(jnp.int32, (CH, CH), 1)
    causal = (columns <= positions).astype(jnp.float32)
    local_state = jnp.einsum('nbchi,nbchj->nbhij', key_heads, value_heads)
    zero_block = jnp.zeros_like(local_state[:, :1])
    prefix_state = jnp.cumsum(jnp.concatenate([zero_block, local_state[:, :-1]], axis=1), axis=1)
    prefix_rounded = rounded(prefix_state)
    block_scores = rounded(jnp.einsum('nbshi,nbthi->nbhst', query_heads, key_heads) * causal)
    attention = jnp.einsum('nbshi,nbhij->nbshj', query_heads, prefix_rounded)
    attention = attention + jnp.einsum('nbhst,nbthj->nbshj', block_scores, value_heads)
    factor = rms_factor(attention)
    normed = (attention * factor).astype(jnp.bfloat16).reshape(sequences * length, features)
    layer_output = jnp.dot(normed, out_weight, preferred_element_type=jnp.float32)
    layer_output = layer_output.astype(jnp.bfloat16).reshape(sequences, length, -1)
    cotangent = out_cotangent.reshape(sequences * length, -1)
    normed_grad = jnp.dot(cotangent, out_weight.T, preferred_element_type=jnp.float32)
    normed_grad = normed_grad.reshape(sequences, blocks, CH, HEADS, HS)
    mean_term = lax.optimization_barrier(jnp.mean(attention * normed_grad, axis=-1, keepdims=True))
    attention_grad = rounded(factor * normed_grad - attention * (factor * factor * factor) * mean_term)
    grad_scores = rounded(jnp.einsum('nbshj,nbthj->nbhst', attention_grad, value_heads) * causal)
    local_grad = jnp.einsum('nbchi,nbchj->nbhij', query_heads, attention_grad)
    shifted = jnp.concatenate([local_grad[:, 1:], zero_block], axis=1)
    suffix_state = jnp.flip(jnp.cumsum(jnp.flip(shifted, axis=1), axis=1), axis=1)
    suffix_rounded = rounded(suffix_state)
    query_grad = jnp.einsum('nbshj,nbhij->nbshi', attention_grad, prefix_rounded)
    query_grad = query_grad + jnp.einsum('nbhst,nbthi->nbshi', grad_scores, key_heads)
    key_grad = jnp.einsum('nbthj,nbhij->nbthi', value_heads, suffix_rounded)
    key_grad = key_grad + jnp.einsum('nbhst,nbshi->nbthi', grad_scores, query_heads)
    value_grad = jnp.einsum('nbthi,nbhij->nbthj', key_heads, suffix_rounded)
    value_grad = value_grad + jnp.einsum('nbhst,nbshj->nbthj', block_scores, attention_grad)

    def finish(tensor):
        return tensor.astype(jnp.bfloat16).reshape(sequences, length, features)
    return (layer_output, finish(query_grad), finish(key_grad), finish(value_grad))
```

```python
import functools

import jax
import jax.numpy as jnp
from jax import lax
from jax.experimental import pallas as pl
from jax.experimental.pallas import tpu as pltpu
from jax.sharding import PartitionSpec as P

HS = 128


def carried_in(value, axis, join, neutral):
    count, mine = (lax.axis_size(axis), lax.axis_index(axis))
    pieces = lax.all_gather(value, axis)
    total = jnp.full_like(value, 0) + jnp.asarray(neutral, value.dtype)

    def step(position, total):
        longer = join(total, pieces[position])
        return jnp.where(position < mine, longer, total)

    return lax.fori_loop(0, count - 1, step, total)


def prefix(shard, axis, join, neutral):
    count = lax.axis_size(axis)
    place = lax.axis_index(axis)
    ahead = count - 1 - place
    gathered = lax.all_gather(shard.astype(jnp.bfloat16), axis)
    state = jnp.zeros_like(shard) + jnp.asarray(neutral, shard.dtype)

    def one(step, state):
        source = count - 1 - step
        return join(state, lax.dynamic_index_in_dim(gathered, source, 0, False).astype(shard.dtype))

    return lax.fori_loop(0, ahead, one, state)


def add_states(earlier, later):
    return earlier + later


def rms_factor(attention):
    return lax.rsqrt(jnp.mean(attention * attention, axis=-1, keepdims=True) + 1e-05)


def causal_mask(positions_count):
    positions = lax.broadcasted_iota(jnp.int32, (positions_count, positions_count), 0)
    columns = lax.broadcasted_iota(jnp.int32, (positions_count, positions_count), 1)
    return (columns <= positions).astype(jnp.float32)


def local(queries, key_vectors, value_vectors, out_weight, out_cotangent):
    positions_count = queries.shape[1]
    features = queries.shape[2]
    head_count = features // HS
    query_heads = queries[0].reshape(positions_count, head_count, HS)
    key_heads = key_vectors[0].reshape(positions_count, head_count, HS)
    value_heads = value_vectors[0].reshape(positions_count, head_count, HS)
    causal = causal_mask(positions_count)
    local_state = jnp.einsum(
        "chi,chj->hij", key_heads, value_heads, preferred_element_type=jnp.float32
    )
    prefix_state = carried_in(local_state, "seq", add_states, jnp.zeros_like(local_state))
    prefix_rounded = prefix_state.astype(jnp.bfloat16)
    block_scores = jnp.einsum(
        "shi,thi->hst", query_heads, key_heads, preferred_element_type=jnp.float32
    )
    block_scores = (block_scores * causal).astype(jnp.bfloat16)
    attention = jnp.einsum(
        "shi,hij->shj", query_heads, prefix_rounded, preferred_element_type=jnp.float32
    )
    attention = attention + jnp.einsum(
        "hst,thj->shj", block_scores, value_heads, preferred_element_type=jnp.float32
    )
    factor = rms_factor(attention)
    normed = (attention * factor).astype(jnp.bfloat16).reshape(positions_count, features)
    cotangent = out_cotangent[0]
    weight_piece = lax.all_gather(out_weight, ("seq", "dp"), axis=1, tiled=True)
    product = jnp.dot(normed, weight_piece, preferred_element_type=jnp.float32)
    output_part = product
    normed_grad = lax.dot_general(
        cotangent, weight_piece, (((1,), (1,)), ((), ())), preferred_element_type=jnp.float32
    )
    output_part, normed_grad = (output_part, normed_grad)
    layer_output = lax.psum_scatter(
        output_part.astype(jnp.bfloat16), "sub", scatter_dimension=1, tiled=True
    )[None]
    grad_heads = normed_grad.reshape(positions_count, head_count, HS)
    mean_term = jnp.mean(attention * grad_heads, axis=-1, keepdims=True)
    attention_grad = (
        factor * grad_heads - attention * (factor * factor * factor) * mean_term
    ).astype(jnp.bfloat16)
    grad_scores = jnp.einsum(
        "shj,thj->hst", attention_grad, value_heads, preferred_element_type=jnp.float32
    )
    grad_scores = (grad_scores * causal).astype(jnp.bfloat16)
    local_grad = jnp.einsum(
        "chi,chj->hij", query_heads, attention_grad, preferred_element_type=jnp.float32
    )
    suffix_state = prefix(local_grad, "seq", add_states, jnp.zeros_like(local_grad))
    suffix_rounded = suffix_state.astype(jnp.bfloat16)
    query_grad = jnp.einsum(
        "shj,hij->shi", attention_grad, prefix_rounded, preferred_element_type=jnp.float32
    )
    query_grad = query_grad + jnp.einsum(
        "hst,thi->shi", grad_scores, key_heads, preferred_element_type=jnp.float32
    )
    key_grad = jnp.einsum(
        "thj,hij->thi", value_heads, suffix_rounded, preferred_element_type=jnp.float32
    )
    key_grad = key_grad + jnp.einsum(
        "hst,shi->thi", grad_scores, query_heads, preferred_element_type=jnp.float32
    )
    value_grad = jnp.einsum(
        "thi,hij->thj", key_heads, suffix_rounded, preferred_element_type=jnp.float32
    )
    value_grad = value_grad + jnp.einsum(
        "hst,shj->thj", block_scores, attention_grad, preferred_element_type=jnp.float32
    )

    def finish(tensor):
        return tensor.astype(jnp.bfloat16).reshape(1, positions_count, features)

    return (layer_output, finish(query_grad), finish(key_grad), finish(value_grad))


MESH = pl.DeviceIdType.MESH
F32, BF16 = jnp.float32, jnp.bfloat16
CHUNKS = 4


def dot(a, b, ca, cb):
    return lax.dot_general(a, b, (((ca,), (cb,)), ((), ())), preferred_element_type=F32)


def body(nz, head_count, rows, wd, *refs):
    (q_in, k_in, v_in, w, cot, out, qg, kg, vg, wg, cotg, lst, pin, pout, scores, att, normg, acc, ngs, ngr,
     osend, orecv, oacc, ofin, oin, ag, kloc, vloc, sin, sout,
     q, k, v, in_sem, own_sem, wu_s, wu_r, wd_s, wd_r, c_s, c_r, p_s, p_r, x_s, x_r, n_s, n_r, g_s, g_r, o_s, o_r, f_s, f_r) = refs
    z, x = lax.axis_index("seq"), lax.axis_index("dp")
    y, s = lax.axis_index("groups"), lax.axis_index("sub")
    half, hb, feat = wd // 2, nz // 2, head_count * HS
    per = head_count // CHUNKS
    has_up, has_down = z < nz - 1, z > 0

    def place(j):
        return lax.rem(x + (j & 1), 2), lax.rem(y + (j >> 1), 2)

    def to_peer(j):
        xj, yj = place(j)
        return {"dp": xj, "groups": yj}

    def remote(src, dst, send, recv, device):
        return pltpu.make_async_remote_copy(
            src_ref=src, dst_ref=dst, send_sem=send, recv_sem=recv, device_id=device, device_id_type=MESH)

    up, down = {"seq": jnp.minimum(z + 1, nz - 1)}, {"seq": jnp.maximum(z - 1, 0)}
    other = {"sub": 1 - s}

    loads = [pltpu.make_async_copy(a, b, in_sem.at[i]) for i, (a, b) in enumerate(((k_in, k), (v_in, v), (q_in, q)))]
    for load in loads:
        load.start()

    barrier = pltpu.get_barrier_semaphore()
    for j in (1, 2, 3):
        pl.semaphore_signal(barrier, inc=1, device_id=to_peer(j), device_id_type=MESH)
    pl.semaphore_signal(barrier, inc=1, device_id=other, device_id_type=MESH)

    @pl.when(has_up)
    def _():
        pl.semaphore_signal(barrier, inc=1, device_id=up, device_id_type=MESH)

    @pl.when(has_down)
    def _():
        pl.semaphore_signal(barrier, inc=1, device_id=down, device_id_type=MESH)
    pl.semaphore_wait(barrier, 4 + has_up.astype(jnp.int32) + has_down.astype(jnp.int32))

    mine = w.at[:, pl.ds(pl.multiple_of(y * half, 128), half)]
    deep = feat // CHUNKS

    def source(block, d, c):
        held = mine if d == 0 else wg.at[block]
        return held.at[c * deep:(c + 1) * deep]

    def up_copy(block, d, c):
        return remote(source(block, d, c), wg.at[block, c * deep:(c + 1) * deep], wu_s.at[d, c], wu_r.at[d, c], up)

    def down_copy(block, d, c):
        return remote(source(block, d, c), wg.at[block, c * deep:(c + 1) * deep], wd_s.at[d, c], wd_r.at[d, c], down)

    def start_own(c):
        @pl.when(has_up)
        def _():
            up_copy(z, 0, c).start()

        @pl.when((z < nz - 1) & has_down)
        def _():
            down_copy(z, 0, c).start()

    start_own(0)

    @pl.when(z == nz - 1)
    def _():
        for c in range(CHUNKS):
            down_copy(z, 0, c).start()
    own_w = pltpu.make_async_copy(mine, wg.at[z], own_sem.at[nz])
    own_w.start()

    def cot_piece(j, b):
        xj, yj = place(j)
        return cot.at[0, :, pl.ds(pl.multiple_of((b * 2 + xj) * wd + yj * half, 128), half)]

    def cot_own(b):
        return pltpu.make_async_copy(cot_piece(0, b), cotg.at[b, 0], own_sem.at[b])

    def cot_copy(j, b):
        return remote(cot_piece(j, b), cotg.at[b, j], c_s.at[j, b], c_r.at[j, b], to_peer(j))

    for b in range(nz):
        cot_own(b).start()
        for j in (1, 2, 3):
            cot_copy(j, b).start()

    def col(h):
        return slice(h * HS, (h + 1) * HS)

    def prefix_copy(g):
        part = pl.ds(g * per, per)
        return remote(pout.at[part], pin.at[part], p_s.at[g], p_r.at[g], up)

    def suffix_copy(g):
        part = pl.ds(g * per, per)
        return remote(sout.at[part], sin.at[part], x_s.at[g], x_r.at[g], down)

    for load in loads:
        load.wait()
    for g in range(CHUNKS):
        for h in range(g * per, (g + 1) * per):
            lst[h] = dot(k[0, :, col(h)], v[0, :, col(h)], 0, 0)

        @pl.when(z == 0)
        def _():
            part = slice(g * per, (g + 1) * per)
            pout[part] = lst[part].astype(BF16)
            pin[part] = jnp.zeros((per, HS, HS), BF16)
            prefix_copy(g).start()

    causal = (lax.broadcasted_iota(jnp.int32, (rows, rows), 1) <= lax.broadcasted_iota(jnp.int32, (rows, rows), 0))
    for h in range(head_count):
        product = dot(q[0, :, col(h)], k[0, :, col(h)], 1, 1)
        scores[h] = jnp.where(causal, product, 0.0).astype(BF16)
    for h in range(head_count):
        att[h] = dot(scores[h], v[0, :, col(h)], 1, 0)

    def normed_copy(j):
        return remote(normg.at[0], normg.at[j], n_s.at[j], n_r.at[j], to_peer(j))

    def grad_copy(j, c):
        part = slice(c * deep, (c + 1) * deep)
        return remote(ngs.at[j, :, part], ngr.at[j, :, part], g_s.at[j, c], g_r.at[j, c], to_peer(j))

    def attend():
        @pl.when(z > 0)
        def _():
            for g in range(CHUNKS):
                prefix_copy(g).wait_recv()

                @pl.when(has_up)
                def _():
                    part = slice(g * per, (g + 1) * per)
                    pout[part] = (pin[part].astype(F32) + lst[part]).astype(BF16)
                    prefix_copy(g).start()

        for h in range(head_count):
            total = att[h] + dot(q[0, :, col(h)], pin[h], 1, 0)
            att[h] = total
            factor = lax.rsqrt(jnp.mean(total * total, axis=-1, keepdims=True) + 1e-05)
            normg[0, :, col(h)] = (total * factor).astype(BF16)
        for j in (1, 2, 3):
            normed_copy(j).start()

    def turn(g):
        for j in (1, 2, 3):
            grad_copy(j, g).wait_recv()
        for h in range(g * per, (g + 1) * per):
            grad = acc[:, col(h)]
            for j in (1, 2, 3):
                grad = grad + ngr[j, :, col(h)].astype(F32)
            total = att[h]
            factor = lax.rsqrt(jnp.mean(total * total, axis=-1, keepdims=True) + 1e-05)
            mean_term = jnp.mean(total * grad, axis=-1, keepdims=True)
            turned = (factor * grad - total * (factor * factor * factor) * mean_term).astype(BF16)
            ag[h] = turned
            lst[h] = dot(q[0, :, col(h)], turned, 0, 0)

        @pl.when(z == nz - 1)
        def _():
            part = slice(g * per, (g + 1) * per)
            sout[part] = lst[part].astype(BF16)
            sin[part] = jnp.zeros((per, HS, HS), BF16)
            suffix_copy(g).start()

    for c in range(CHUNKS):
        if c + 1 < CHUNKS:
            start_own(c + 1)
        for d in range(1, nz):
            @pl.when(z - d >= 0)
            def _():
                up_copy(z - d, d - 1, c).wait_recv()

                @pl.when(has_up)
                def _():
                    up_copy(z - d, d, c).start()

            @pl.when(z + d < nz)
            def _():
                down_copy(z + d, d - 1, c).wait_recv()

                @pl.when(has_down)
                def _():
                    down_copy(z + d, d, c).start()
        if c == 0:
            own_w.wait()
            for b in range(nz):
                cot_own(b).wait()
                for j in (1, 2, 3):
                    cot_copy(j, b).wait_recv()
        part = slice(c * deep, (c + 1) * deep)
        total = dot(cotg[0].reshape(4 * rows, half), wg[0, part, :], 1, 1)
        for b in range(1, nz):
            total = total + dot(cotg[b].reshape(4 * rows, half), wg[b, part, :], 1, 1)
        acc[:, part] = total[:rows]
        for j in (1, 2, 3):
            ngs[j, :, part] = total[j * rows:(j + 1) * rows].astype(BF16)
            grad_copy(j, c).start()
        if c == 0:
            @pl.when(z <= 1)
            def _():
                attend()
        elif c < CHUNKS - 1:
            @pl.when(z == c + 1)
            def _():
                attend()
        if c == CHUNKS - 2:
            turn(0)
        if c == CHUNKS - 1:
            for g in range(1, CHUNKS - 1):
                turn(g)

    for j in (1, 2, 3):
        normed_copy(j).wait_recv()
    sub_copy = remote(osend, orecv, o_s.at[0], o_r.at[0], other)

    @pl.loop(0, hb)
    def _(i):
        left = normg[...].reshape(4 * rows, feat)
        osend[i] = dot(left, wg[(1 - s) * hb + i], 1, 0).astype(BF16).reshape(4, rows, half)
    sub_copy.start()

    @pl.loop(0, hb)
    def _(i):
        left = normg[...].reshape(4 * rows, feat)
        oacc[i] = dot(left, wg[s * hb + i], 1, 0).reshape(4, rows, half)

    turn(CHUNKS - 1)

    def out_copy(i, j):
        return remote(ofin.at[i, j], oin.at[i, j], f_s.at[i, j], f_r.at[i, j], to_peer(j))

    sub_copy.wait_recv()
    for i in range(hb):
        ofin[i] = (oacc[i] + orecv[i].astype(F32)).astype(BF16)
        for j in (1, 2, 3):
            out_copy(i, j).start()

    for h in range(head_count):
        turned = ag[h]
        grad_scores = jnp.where(causal, dot(turned, v[0, :, col(h)], 1, 1), 0.0).astype(BF16)
        qg[0, :, col(h)] = (dot(turned, pin[h], 1, 1) + dot(grad_scores, k[0, :, col(h)], 1, 0)).astype(BF16)
        kloc[h] = dot(grad_scores, q[0, :, col(h)], 0, 0)
        vloc[h] = dot(scores[h], turned, 0, 0)

    @pl.when(has_up)
    def _():
        for g in range(CHUNKS):
            suffix_copy(g).wait_recv()

            @pl.when(has_down)
            def _():
                part = slice(g * per, (g + 1) * per)
                sout[part] = (sin[part].astype(F32) + lst[part]).astype(BF16)
                suffix_copy(g).start()

    for h in range(head_count):
        kg[0, :, col(h)] = (kloc[h] + dot(v[0, :, col(h)], sin[h], 1, 1)).astype(BF16)
        vg[0, :, col(h)] = (vloc[h] + dot(k[0, :, col(h)], sin[h], 1, 0)).astype(BF16)

    for i in range(hb):
        for j in range(4):
            xj, yj = place(j)
            part = pl.ds(pl.multiple_of((i * 2 + xj) * wd + yj * half, 128), half)
            if j == 0:
                out[0, :, part] = ofin[i, 0]
            else:
                out_copy(i, j).wait_recv()
                out[0, :, part] = oin[i, j]

    for c in range(CHUNKS):
        for d in range(nz - 1):
            @pl.when(has_up & (z - d >= 0))
            def _():
                up_copy(z, d, c).wait_send()

            @pl.when(has_down & (z + d < nz))
            def _():
                down_copy(z, d, c).wait_send()

    for g in range(CHUNKS):
        @pl.when(has_up)
        def _():
            prefix_copy(g).wait_send()

        @pl.when(has_down)
        def _():
            suffix_copy(g).wait_send()
    for j in (1, 2, 3):
        for b in range(nz):
            cot_copy(j, b).wait_send()
        normed_copy(j).wait_send()
        for c in range(CHUNKS):
            grad_copy(j, c).wait_send()
        for i in range(hb):
            out_copy(i, j).wait_send()
    sub_copy.wait_send()


def hand_over(*refs):
    copies = [pltpu.make_async_copy(refs[i], refs[4 + i], refs[8].at[i]) for i in range(4)]
    for copy in copies:
        copy.start()
    for copy in copies:
        copy.wait()


def fused(nz, queries, key_vectors, value_vectors, out_weight, out_cotangent):
    rows, feat = queries.shape[1:]
    wd = out_weight.shape[1]
    heads, half, hb = feat // HS, wd // 2, nz // 2
    vmem, dma = pltpu.VMEM, pltpu.SemaphoreType.DMA
    states = (heads, HS, HS)
    inside = pl.BlockSpec(memory_space=pltpu.VMEM)
    outside = pl.BlockSpec(memory_space=pltpu.HBM)
    grads = pltpu.VMEM((1, rows, feat), BF16)
    outs = pl.pallas_call(
        functools.partial(body, nz, heads, rows, wd),
        out_shape=(pltpu.VMEM((1, rows, nz * wd), BF16), grads, grads, grads),
        in_specs=[outside] * 5,
        out_specs=(inside,) * 4,
        scratch_shapes=[
            vmem((nz, feat, half), BF16), vmem((nz, 4, rows, half), BF16),
            vmem(states, F32), vmem(states, BF16), vmem(states, BF16),
            vmem((heads, rows, rows), BF16), vmem((heads, rows, HS), F32),
            vmem((4, rows, feat), BF16), vmem((rows, feat), F32),
            vmem((4, rows, feat), BF16), vmem((4, rows, feat), BF16),
            vmem((hb, 4, rows, half), BF16), vmem((hb, 4, rows, half), BF16),
            vmem((hb, 4, rows, half), F32), vmem((hb, 4, rows, half), BF16), vmem((hb, 4, rows, half), BF16),
            vmem((heads, rows, HS), BF16), vmem((heads, rows, HS), F32), vmem((heads, rows, HS), F32),
            vmem(states, BF16), vmem(states, BF16),
            vmem((1, rows, feat), BF16), vmem((1, rows, feat), BF16), vmem((1, rows, feat), BF16), dma((3,)),
            dma((nz + 1,)), dma((nz, CHUNKS)), dma((nz, CHUNKS)), dma((nz, CHUNKS)), dma((nz, CHUNKS)),
            dma((4, nz)), dma((4, nz)), dma((CHUNKS,)), dma((CHUNKS,)), dma((CHUNKS,)), dma((CHUNKS,)),
            dma((4,)), dma((4,)), dma((4, CHUNKS)), dma((4, CHUNKS)), dma((1,)), dma((1,)), dma((hb, 4)), dma((hb, 4)),
        ],
        compiler_params=pltpu.CompilerParams(
            collective_id=0, has_side_effects=True, vmem_limit_bytes=60 * 1024 * 1024),
    )(queries, key_vectors, value_vectors, out_weight, out_cotangent)
    grads = jax.ShapeDtypeStruct((1, rows, feat), BF16)
    return tuple(pl.pallas_call(
        hand_over,
        out_shape=(jax.ShapeDtypeStruct((1, rows, nz * wd), BF16), grads, grads, grads),
        in_specs=[pl.BlockSpec(memory_space=pltpu.VMEM)] * 4,
        out_specs=(outside,) * 4,
        scratch_shapes=[dma((4,))],
    )(*(pltpu.with_memory_space_constraint(o, pltpu.VMEM) for o in outs)))


def solution(mesh):
    placed = (
        P(("groups", "dp"), "seq", "sub"),
        P(("groups", "dp"), "seq", "sub"),
        P(("groups", "dp"), "seq", "sub"),
        P("sub", ("seq", "dp")),
        P(("groups", "dp"), "seq", None),
    )
    shape = dict(mesh.shape)
    count = shape["seq"]

    def part(queries, key_vectors, value_vectors, out_weight, out_cotangent):
        args = (queries, key_vectors, value_vectors, out_weight, out_cotangent)
        fits = shape["groups"] == shape["dp"] == shape["sub"] == 2 and count % 2 == 0
        if fits and count <= 4 and out_weight.shape[1] % 256 == 0:
            return fused(count, *args)
        return local(*args)

    return jax.shard_map(
        part,
        mesh=mesh,
        in_specs=placed,
        out_specs=(
            P(("groups", "dp"), "seq", "sub"),
            P(("groups", "dp"), "seq", "sub"),
            P(("groups", "dp"), "seq", "sub"),
            P(("groups", "dp"), "seq", "sub"),
        ),
        check_vma=False,
    )
```

```python
import functools

import jax
import jax.numpy as jnp
from jax import lax
from jax.experimental import pallas as pl
from jax.experimental.pallas import tpu as pltpu
from jax.sharding import PartitionSpec as P

HS = 128


def carried_in(value, axis, join, neutral):
    count, mine = (lax.axis_size(axis), lax.axis_index(axis))
    pieces = lax.all_gather(value, axis)
    total = jnp.full_like(value, 0) + jnp.asarray(neutral, value.dtype)

    def step(position, total):
        longer = join(total, pieces[position])
        return jnp.where(position < mine, longer, total)

    return lax.fori_loop(0, count - 1, step, total)


def prefix(shard, axis, join, neutral):
    count = lax.axis_size(axis)
    place = lax.axis_index(axis)
    ahead = count - 1 - place
    gathered = lax.all_gather(shard.astype(jnp.bfloat16), axis)
    state = jnp.zeros_like(shard) + jnp.asarray(neutral, shard.dtype)

    def one(step, state):
        source = count - 1 - step
        return join(state, lax.dynamic_index_in_dim(gathered, source, 0, False).astype(shard.dtype))

    return lax.fori_loop(0, ahead, one, state)


def add_states(earlier, later):
    return earlier + later


def rms_factor(attention):
    return lax.rsqrt(jnp.mean(attention * attention, axis=-1, keepdims=True) + 1e-05)


def causal_mask(positions_count):
    positions = lax.broadcasted_iota(jnp.int32, (positions_count, positions_count), 0)
    columns = lax.broadcasted_iota(jnp.int32, (positions_count, positions_count), 1)
    return (columns <= positions).astype(jnp.float32)


def local(queries, key_vectors, value_vectors, out_weight, out_cotangent):
    positions_count = queries.shape[1]
    features = queries.shape[2]
    head_count = features // HS
    query_heads = queries[0].reshape(positions_count, head_count, HS)
    key_heads = key_vectors[0].reshape(positions_count, head_count, HS)
    value_heads = value_vectors[0].reshape(positions_count, head_count, HS)
    causal = causal_mask(positions_count)
    local_state = jnp.einsum(
        "chi,chj->hij", key_heads, value_heads, preferred_element_type=jnp.float32
    )
    prefix_state = carried_in(local_state, "seq", add_states, jnp.zeros_like(local_state))
    prefix_rounded = prefix_state.astype(jnp.bfloat16)
    block_scores = jnp.einsum(
        "shi,thi->hst", query_heads, key_heads, preferred_element_type=jnp.float32
    )
    block_scores = (block_scores * causal).astype(jnp.bfloat16)
    attention = jnp.einsum(
        "shi,hij->shj", query_heads, prefix_rounded, preferred_element_type=jnp.float32
    )
    attention = attention + jnp.einsum(
        "hst,thj->shj", block_scores, value_heads, preferred_element_type=jnp.float32
    )
    factor = rms_factor(attention)
    normed = (attention * factor).astype(jnp.bfloat16).reshape(positions_count, features)
    cotangent = out_cotangent[0]
    weight_piece = lax.all_gather(out_weight, ("seq", "dp"), axis=1, tiled=True)
    product = jnp.dot(normed, weight_piece, preferred_element_type=jnp.float32)
    output_part = product
    normed_grad = lax.dot_general(
        cotangent, weight_piece, (((1,), (1,)), ((), ())), preferred_element_type=jnp.float32
    )
    output_part, normed_grad = (output_part, normed_grad)
    layer_output = lax.psum_scatter(
        output_part.astype(jnp.bfloat16), "sub", scatter_dimension=1, tiled=True
    )[None]
    grad_heads = normed_grad.reshape(positions_count, head_count, HS)
    mean_term = jnp.mean(attention * grad_heads, axis=-1, keepdims=True)
    attention_grad = (
        factor * grad_heads - attention * (factor * factor * factor) * mean_term
    ).astype(jnp.bfloat16)
    grad_scores = jnp.einsum(
        "shj,thj->hst", attention_grad, value_heads, preferred_element_type=jnp.float32
    )
    grad_scores = (grad_scores * causal).astype(jnp.bfloat16)
    local_grad = jnp.einsum(
        "chi,chj->hij", query_heads, attention_grad, preferred_element_type=jnp.float32
    )
    suffix_state = prefix(local_grad, "seq", add_states, jnp.zeros_like(local_grad))
    suffix_rounded = suffix_state.astype(jnp.bfloat16)
    query_grad = jnp.einsum(
        "shj,hij->shi", attention_grad, prefix_rounded, preferred_element_type=jnp.float32
    )
    query_grad = query_grad + jnp.einsum(
        "hst,thi->shi", grad_scores, key_heads, preferred_element_type=jnp.float32
    )
    key_grad = jnp.einsum(
        "thj,hij->thi", value_heads, suffix_rounded, preferred_element_type=jnp.float32
    )
    key_grad = key_grad + jnp.einsum(
        "hst,shi->thi", grad_scores, query_heads, preferred_element_type=jnp.float32
    )
    value_grad = jnp.einsum(
        "thi,hij->thj", key_heads, suffix_rounded, preferred_element_type=jnp.float32
    )
    value_grad = value_grad + jnp.einsum(
        "hst,shj->thj", block_scores, attention_grad, preferred_element_type=jnp.float32
    )

    def finish(tensor):
        return tensor.astype(jnp.bfloat16).reshape(1, positions_count, features)

    return (layer_output, finish(query_grad), finish(key_grad), finish(value_grad))


MESH = pl.DeviceIdType.MESH
F32, BF16 = jnp.float32, jnp.bfloat16
PIECES = ((0, 2), (2, 2), (4, 2), (6, 1), (7, 1))
GROUPS = 4
EARLY = 6


def dot(a, b, ca, cb):
    return lax.dot_general(a, b, (((ca,), (cb,)), ((), ())), preferred_element_type=F32)


def body(nz, head_count, rows, wd, *refs):
    (q_in, k_in, v_in, w, cot, out, qg, kg, vg, wg, cotg, lst, pin, pout, scores, att, normg, acc, ngs, ngr,
     osend, orecv, oacc, ofin, ag, kloc, vloc, near, far, sout,
     q, k, v, in_sem, own_sem, w_s, w_r, c_s, c_r, p_s, p_r, a_s, a_r, b_s, b_r, n_s, n_r, g_s, g_r, o_s, o_r, f_s, f_r) = refs
    z, x = lax.axis_index("seq"), lax.axis_index("dp")
    y, s = lax.axis_index("groups"), lax.axis_index("sub")
    half, hb, feat = wd // 2, nz // 2, head_count * HS
    per = head_count // GROUPS
    last = nz - 1
    peers = (1, 2, 3)

    def place(j):
        return lax.rem(x + (j & 1), 2), lax.rem(y + (j >> 1), 2)

    def to_peer(j):
        xj, yj = place(j)
        return {"dp": xj, "groups": yj}

    def remote(src, dst, send, recv, device):
        return pltpu.make_async_remote_copy(
            src_ref=src, dst_ref=dst, send_sem=send, recv_sem=recv, device_id=device, device_id_type=MESH)

    other = {"sub": 1 - s}

    loads = [pltpu.make_async_copy(a, b, in_sem.at[i]) for i, (a, b) in enumerate(((k_in, k), (v_in, v), (q_in, q)))]
    for load in loads:
        load.start()

    barrier = pltpu.get_barrier_semaphore()
    for j in peers:
        pl.semaphore_signal(barrier, inc=1, device_id=to_peer(j), device_id_type=MESH)
    for d in range(1, nz):
        pl.semaphore_signal(barrier, inc=1, device_id={"seq": lax.rem(z + d, nz)}, device_id_type=MESH)
    pl.semaphore_signal(barrier, inc=1, device_id=other, device_id_type=MESH)
    pl.semaphore_wait(barrier, nz + 3)

    mine = w.at[:, pl.ds(pl.multiple_of(y * half, 128), half)]
    sent = {zz: [] for zz in range(nz)}

    def span(c):
        first, count = PIECES[c]
        return slice(first * HS, (first + count) * HS)

    def w_copy(zz, block, c, dz):
        src = mine if block == zz else wg.at[block]
        return remote(src.at[span(c)], wg.at[block, span(c)], w_s.at[(dz + 1) // 2, block, c], w_r.at[block, c], {"seq": zz + dz})

    def prefix_copy(zz, g):
        part = pl.ds(g * per, per)
        return remote(pout.at[part], pin.at[part], p_s.at[g], p_r.at[g], {"seq": zz + 1})

    def heads_of(c):
        first, count = PIECES[c]
        return pl.ds(first, count)

    def near_copy(zz, c):
        return remote(sout.at[heads_of(c)], near.at[heads_of(c)], a_s.at[c], a_r.at[c], {"seq": zz - 1})

    def far_copy(to, c):
        return remote(sout.at[heads_of(c)], far.at[heads_of(c)], b_s.at[to, c], b_r.at[c], {"seq": to})

    def stage(table):
        for zz, ops in table.items():
            @pl.when(z == zz)
            def _():
                for op in ops:
                    if op[0] == "w":
                        copy = w_copy(zz, *op[1:])
                        if op[1] != zz:
                            w_copy(zz, op[1], op[2], op[3]).wait_recv()
                        copy.start()
                        sent[zz].append((w_copy, op[1:]))
                    elif op[0] == "p":
                        g = op[1]
                        part = slice(g * per, (g + 1) * per)
                        copy = prefix_copy(min(zz, last - 1), g)
                        if zz > 0:
                            copy.wait_recv()
                        if zz == 0:
                            pout[part] = lst[part].astype(BF16)
                            pin[part] = jnp.zeros((per, HS, HS), BF16)
                        elif zz < last:
                            pout[part] = (pin[part].astype(F32) + lst[part]).astype(BF16)
                        if zz < last:
                            copy.start()
                            sent[zz].append((prefix_copy, (g,)))

    def own(c, *ways):
        return [("w", None, c, way) for way in ways]

    def table(**rows_of):
        made = {}
        for name, ops in rows_of.items():
            zz = int(name[1:])
            made[zz] = [tuple(zz if (i == 1 and part is None) else part for i, part in enumerate(op)) for op in ops]
        return made

    stage(table(
        z0=own(0, 1),
        z1=own(0, 1, -1) + own(1, 1, -1),
        z2=own(0, 1, -1) + own(1, 1, -1),
        z3=[op for c in range(len(PIECES)) for op in own(c, -1)],
    ))
    own_w = pltpu.make_async_copy(mine, wg.at[z], own_sem.at[nz])
    own_w.start()

    def cot_piece(j, b):
        xj, yj = place(j)
        return cot.at[0, :, pl.ds(pl.multiple_of((b * 2 + xj) * wd + yj * half, 128), half)]

    def cot_own(b):
        return pltpu.make_async_copy(cot_piece(0, b), cotg.at[b, 0], own_sem.at[b])

    def cot_copy(j, b):
        return remote(cot_piece(j, b), cotg.at[b, j], c_s.at[j, b], c_r.at[j, b], to_peer(j))

    for b in range(nz):
        cot_own(b).start()
        for j in peers:
            cot_copy(j, b).start()

    def col(h):
        return slice(h * HS, (h + 1) * HS)

    for load in loads:
        load.wait()
    for h in range(head_count):
        lst[h] = dot(k[0, :, col(h)], v[0, :, col(h)], 0, 0)
    stage(table(
        z0=[("p", g) for g in range(GROUPS)] + [op for c in range(1, len(PIECES)) for op in own(c, 1)],
    ))

    @pl.when(z >= 2)
    def _():
        near[...] = jnp.zeros(near.shape, BF16)

    @pl.when(z == last)
    def _():
        far[...] = jnp.zeros(far.shape, BF16)

    causal = (lax.broadcasted_iota(jnp.int32, (rows, rows), 1) <= lax.broadcasted_iota(jnp.int32, (rows, rows), 0))
    for h in range(head_count):
        product = dot(q[0, :, col(h)], k[0, :, col(h)], 1, 1)
        scores[h] = jnp.where(causal, product, 0.0).astype(BF16)
    for h in range(head_count):
        att[h] = dot(scores[h], v[0, :, col(h)], 1, 0)

    def normed_copy(j, g):
        part = slice(g * per * HS, (g + 1) * per * HS)
        return remote(normg.at[0, :, part], normg.at[j, :, part], n_s.at[j, g], n_r.at[j, g], to_peer(j))

    def grad_copy(j, c):
        return remote(ngs.at[j, :, span(c)], ngr.at[j, :, span(c)], g_s.at[j, c], g_r.at[j, c], to_peer(j))

    def attend(g):
        for h in range(g * per, (g + 1) * per):
            total = att[h] + dot(q[0, :, col(h)], pin[h], 1, 0)
            att[h] = total
            factor = lax.rsqrt(jnp.mean(total * total, axis=-1, keepdims=True) + 1e-05)
            normg[0, :, col(h)] = (total * factor).astype(BF16)
        for j in peers:
            normed_copy(j, g).start()

    def gradient(c):
        for zz in (0, last):
            @pl.when(z == zz)
            def _():
                for b in range(nz):
                    if b != zz:
                        w_copy(zz, b, c, 1 if zz == 0 else -1).wait_recv()
        part = span(c)
        total = dot(cotg[0].reshape(4 * rows, half), wg[0, part, :], 1, 1)
        for b in range(1, nz):
            total = total + dot(cotg[b].reshape(4 * rows, half), wg[b, part, :], 1, 1)
        acc[:, part] = total[:rows]
        for j in peers:
            ngs[j, :, part] = total[j * rows:(j + 1) * rows].astype(BF16)
            grad_copy(j, c).start()

    def turn(c):
        for j in peers:
            grad_copy(j, c).wait_recv()
        first, count = PIECES[c]
        for h in range(first, first + count):
            grad = acc[:, col(h)]
            for j in peers:
                grad = grad + ngr[j, :, col(h)].astype(F32)
            total = att[h]
            factor = lax.rsqrt(jnp.mean(total * total, axis=-1, keepdims=True) + 1e-05)
            mean_term = jnp.mean(total * grad, axis=-1, keepdims=True)
            turned = (factor * grad - total * (factor * factor * factor) * mean_term).astype(BF16)
            ag[h] = turned
            lst[h] = dot(q[0, :, col(h)], turned, 0, 0)
            sout[h] = lst[h].astype(BF16)

        @pl.when(z == last)
        def _():
            for to in range(last):
                far_copy(to, c).start()

        @pl.when(z == 2)
        def _():
            near_copy(2, c).start()

    def finish(c):
        first, count = PIECES[c]
        for h in range(first, first + count):
            turned = ag[h]
            grad_scores = jnp.where(causal, dot(turned, v[0, :, col(h)], 1, 1), 0.0).astype(BF16)
            qg[0, :, col(h)] = (dot(turned, pin[h], 1, 1) + dot(grad_scores, k[0, :, col(h)], 1, 0)).astype(BF16)
            kloc[h] = dot(grad_scores, q[0, :, col(h)], 0, 0)
            vloc[h] = dot(scores[h], turned, 0, 0)

    def up(block, c):
        return ("w", block, c, 1)

    def down(block, c):
        return ("w", block, c, -1)

    stage(table(
        z1=[up(0, 0), down(2, 0)],
        z2=[up(1, 0), down(3, 0)],
    ))
    for g in range(GROUPS):
        stage(table(
            z1=[("p", g)] + ([down(2, 1)] if g == 0 else [down(3, 0)] if g == GROUPS - 1 else []),
            z2=([up(1, 1), down(3, 1), up(0, 0)] + own(2, -1) if g == 0 else []) + [("p", g)],
            z3=[("p", g)],
        ))
        attend(g)
    stage(table(
        z1=[up(0, 1), down(3, 1)] + own(2, 1, -1),
        z2=[down(3, 2)] + own(3, -1) + [up(0, 1)] + own(2, 1),
    ))
    own_w.wait()
    for b in range(nz):
        cot_own(b).wait()
        for j in peers:
            cot_copy(j, b).wait_recv()
    gradient(0)
    stage(table(
        z1=[up(0, 2), down(2, 2), down(3, 2)] + own(3, 1, -1),
        z2=[down(3, 3), up(1, 2), up(0, 2)] + own(3, 1),
    ))
    gradient(1)
    stage(table(
        z1=[up(0, 3), down(2, 3), down(3, 3)] + own(4, 1, -1) + [up(0, 4), down(2, 4), down(3, 4)],
        z2=own(4, -1) + [down(3, 4), up(1, 3), up(0, 3)] + own(4, 1) + [up(1, 4), up(0, 4)],
    ))
    gradient(2)
    turn(0)
    for j in peers:
        for g in range(GROUPS):
            normed_copy(j, g).wait_recv()
    deep = EARLY * HS

    @pl.loop(0, nz)
    def _(b):
        left = normg[:, :, :deep].reshape(4 * rows, deep)
        oacc[b] = dot(left, wg[b, :deep], 1, 0).reshape(4, rows, half)

    finish(0)
    gradient(3)
    turn(1)
    finish(1)
    turn(2)
    finish(2)
    gradient(4)

    def sub_copy(i):
        return remote(osend.at[i], orecv.at[i], o_s.at[i], o_r.at[i], other)

    left = normg[:, :, deep:].reshape(4 * rows, feat - deep)
    for i in range(hb):
        there = (1 - s) * hb + i
        osend[i] = (oacc[there] + dot(left, wg[there, deep:], 1, 0).reshape(4, rows, half)).astype(BF16)
        sub_copy(i).start()
    for i in range(hb):
        here = s * hb + i
        oacc[here] = oacc[here] + dot(left, wg[here, deep:], 1, 0).reshape(4, rows, half)
    turn(3)

    def out_part(i, xj, yj):
        return out.at[0, :, pl.ds(pl.multiple_of((i * 2 + xj) * wd + yj * half, 128), half)]

    def out_copy(i, j):
        return remote(ofin.at[i, j], out_part(i, x, y), f_s.at[i, j], f_r.at[i, j], to_peer(j))

    for i in range(hb):
        sub_copy(i).wait_recv()
        ofin[i] = (oacc[s * hb + i] + orecv[i].astype(F32)).astype(BF16)
        for j in peers:
            out_copy(i, j).start()
        out_part(i, x, y)[...] = ofin[i, 0]

    turn(4)

    @pl.when(z == 1)
    def _():
        for c in range(len(PIECES)):
            near_copy(1, c).wait_recv()
            part = heads_of(c)
            sout[part] = (near[part].astype(F32) + lst[part]).astype(BF16)
            near_copy(1, c).start()

    finish(3)
    finish(4)

    for c in range(len(PIECES)):
        @pl.when(z == 0)
        def _():
            near_copy(1, c).wait_recv()

        @pl.when(z < last)
        def _():
            far_copy(0, c).wait_recv()
        first, count = PIECES[c]
        for h in range(first, first + count):
            carried = (near[h].astype(F32) + far[h].astype(F32)).astype(BF16)
            kg[0, :, col(h)] = (kloc[h] + dot(v[0, :, col(h)], carried, 1, 1)).astype(BF16)
            vg[0, :, col(h)] = (vloc[h] + dot(k[0, :, col(h)], carried, 1, 0)).astype(BF16)

    for i in range(hb):
        for j in peers:
            out_copy(i, j).wait_recv()

    for zz in range(nz):
        @pl.when(z == zz)
        def _():
            for make, where in sent[zz]:
                make(zz, *where).wait_send()
            for c in range(len(PIECES)):
                if zz == last:
                    for to in range(last):
                        far_copy(to, c).wait_send()
                elif zz > 0:
                    near_copy(zz, c).wait_send()
    for j in peers:
        for b in range(nz):
            cot_copy(j, b).wait_send()
        for g in range(GROUPS):
            normed_copy(j, g).wait_send()
        for c in range(len(PIECES)):
            grad_copy(j, c).wait_send()
        for i in range(hb):
            out_copy(i, j).wait_send()
    for i in range(hb):
        sub_copy(i).wait_send()


def hand_over(*refs):
    copies = [pltpu.make_async_copy(refs[i], refs[4 + i], refs[8].at[i]) for i in range(4)]
    for copy in copies:
        copy.start()
    for copy in copies:
        copy.wait()


def fused(nz, queries, key_vectors, value_vectors, out_weight, out_cotangent):
    rows, feat = queries.shape[1:]
    wd = out_weight.shape[1]
    heads, half, hb, pieces = feat // HS, wd // 2, nz // 2, len(PIECES)
    vmem, dma = pltpu.VMEM, pltpu.SemaphoreType.DMA
    states = (heads, HS, HS)
    inside = pl.BlockSpec(memory_space=pltpu.VMEM)
    outside = pl.BlockSpec(memory_space=pltpu.HBM)
    grads = pltpu.VMEM((1, rows, feat), BF16)
    outs = pl.pallas_call(
        functools.partial(body, nz, heads, rows, wd),
        out_shape=(pltpu.VMEM((1, rows, nz * wd), BF16), grads, grads, grads),
        in_specs=[outside] * 5,
        out_specs=(inside,) * 4,
        scratch_shapes=[
            vmem((nz, feat, half), BF16), vmem((nz, 4, rows, half), BF16),
            vmem(states, F32), vmem(states, BF16), vmem(states, BF16),
            vmem((heads, rows, rows), BF16), vmem((heads, rows, HS), F32),
            vmem((4, rows, feat), BF16), vmem((rows, feat), F32),
            vmem((4, rows, feat), BF16), vmem((4, rows, feat), BF16),
            vmem((hb, 4, rows, half), BF16), vmem((hb, 4, rows, half), BF16),
            vmem((nz, 4, rows, half), F32), vmem((hb, 4, rows, half), BF16),
            vmem((heads, rows, HS), BF16), vmem((heads, rows, HS), F32), vmem((heads, rows, HS), F32),
            vmem(states, BF16), vmem(states, BF16), vmem(states, BF16),
            vmem((1, rows, feat), BF16), vmem((1, rows, feat), BF16), vmem((1, rows, feat), BF16), dma((3,)),
            dma((nz + 1,)), dma((2, nz, pieces)), dma((nz, pieces)),
            dma((4, nz)), dma((4, nz)), dma((GROUPS,)), dma((GROUPS,)),
            dma((pieces,)), dma((pieces,)), dma((nz, pieces)), dma((pieces,)),
            dma((4, GROUPS)), dma((4, GROUPS)), dma((4, pieces)), dma((4, pieces)),
            dma((hb,)), dma((hb,)), dma((hb, 4)), dma((hb, 4)),
        ],
        compiler_params=pltpu.CompilerParams(
            collective_id=0, has_side_effects=True, vmem_limit_bytes=60 * 1024 * 1024),
    )(queries, key_vectors, value_vectors, out_weight, out_cotangent)
    grads = jax.ShapeDtypeStruct((1, rows, feat), BF16)
    return tuple(pl.pallas_call(
        hand_over,
        out_shape=(jax.ShapeDtypeStruct((1, rows, nz * wd), BF16), grads, grads, grads),
        in_specs=[pl.BlockSpec(memory_space=pltpu.VMEM)] * 4,
        out_specs=(outside,) * 4,
        scratch_shapes=[dma((4,))],
    )(*(pltpu.with_memory_space_constraint(o, pltpu.VMEM) for o in outs)))


def solution(mesh):
    placed = (
        P(("groups", "dp"), "seq", "sub"),
        P(("groups", "dp"), "seq", "sub"),
        P(("groups", "dp"), "seq", "sub"),
        P("sub", ("seq", "dp")),
        P(("groups", "dp"), "seq", None),
    )
    shape = dict(mesh.shape)
    count = shape["seq"]

    def part(queries, key_vectors, value_vectors, out_weight, out_cotangent):
        args = (queries, key_vectors, value_vectors, out_weight, out_cotangent)
        fits = shape["groups"] == shape["dp"] == shape["sub"] == 2 and count == 4
        if fits and queries.shape[2] == 8 * HS and out_weight.shape[1] % 256 == 0:
            return fused(count, *args)
        return local(*args)

    return jax.shard_map(
        part,
        mesh=mesh,
        in_specs=placed,
        out_specs=(
            P(("groups", "dp"), "seq", "sub"),
            P(("groups", "dp"), "seq", "sub"),
            P(("groups", "dp"), "seq", "sub"),
            P(("groups", "dp"), "seq", "sub"),
        ),
        check_vma=False,
    )
```

```python
import functools

import jax
import jax.numpy as jnp
from jax import lax
from jax.experimental import pallas as pl
from jax.experimental.pallas import tpu as pltpu
from jax.sharding import PartitionSpec as P

HS = 128


def carried_in(value, axis, join, neutral):
    count, mine = (lax.axis_size(axis), lax.axis_index(axis))
    pieces = lax.all_gather(value, axis)
    total = jnp.full_like(value, 0) + jnp.asarray(neutral, value.dtype)

    def step(position, total):
        longer = join(total, pieces[position])
        return jnp.where(position < mine, longer, total)

    return lax.fori_loop(0, count - 1, step, total)


def prefix(shard, axis, join, neutral):
    count = lax.axis_size(axis)
    place = lax.axis_index(axis)
    ahead = count - 1 - place
    gathered = lax.all_gather(shard.astype(jnp.bfloat16), axis)
    state = jnp.zeros_like(shard) + jnp.asarray(neutral, shard.dtype)

    def one(step, state):
        source = count - 1 - step
        return join(state, lax.dynamic_index_in_dim(gathered, source, 0, False).astype(shard.dtype))

    return lax.fori_loop(0, ahead, one, state)


def add_states(earlier, later):
    return earlier + later


def rms_factor(attention):
    return lax.rsqrt(jnp.mean(attention * attention, axis=-1, keepdims=True) + 1e-05)


def causal_mask(positions_count):
    positions = lax.broadcasted_iota(jnp.int32, (positions_count, positions_count), 0)
    columns = lax.broadcasted_iota(jnp.int32, (positions_count, positions_count), 1)
    return (columns <= positions).astype(jnp.float32)


def local(queries, key_vectors, value_vectors, out_weight, out_cotangent):
    positions_count = queries.shape[1]
    features = queries.shape[2]
    head_count = features // HS
    query_heads = queries[0].reshape(positions_count, head_count, HS)
    key_heads = key_vectors[0].reshape(positions_count, head_count, HS)
    value_heads = value_vectors[0].reshape(positions_count, head_count, HS)
    causal = causal_mask(positions_count)
    local_state = jnp.einsum(
        "chi,chj->hij", key_heads, value_heads, preferred_element_type=jnp.float32
    )
    prefix_state = carried_in(local_state, "seq", add_states, jnp.zeros_like(local_state))
    prefix_rounded = prefix_state.astype(jnp.bfloat16)
    block_scores = jnp.einsum(
        "shi,thi->hst", query_heads, key_heads, preferred_element_type=jnp.float32
    )
    block_scores = (block_scores * causal).astype(jnp.bfloat16)
    attention = jnp.einsum(
        "shi,hij->shj", query_heads, prefix_rounded, preferred_element_type=jnp.float32
    )
    attention = attention + jnp.einsum(
        "hst,thj->shj", block_scores, value_heads, preferred_element_type=jnp.float32
    )
    factor = rms_factor(attention)
    normed = (attention * factor).astype(jnp.bfloat16).reshape(positions_count, features)
    cotangent = out_cotangent[0]
    weight_piece = lax.all_gather(out_weight, ("seq", "dp"), axis=1, tiled=True)
    product = jnp.dot(normed, weight_piece, preferred_element_type=jnp.float32)
    output_part = product
    normed_grad = lax.dot_general(
        cotangent, weight_piece, (((1,), (1,)), ((), ())), preferred_element_type=jnp.float32
    )
    output_part, normed_grad = (output_part, normed_grad)
    layer_output = lax.psum_scatter(
        output_part.astype(jnp.bfloat16), "sub", scatter_dimension=1, tiled=True
    )[None]
    grad_heads = normed_grad.reshape(positions_count, head_count, HS)
    mean_term = jnp.mean(attention * grad_heads, axis=-1, keepdims=True)
    attention_grad = (
        factor * grad_heads - attention * (factor * factor * factor) * mean_term
    ).astype(jnp.bfloat16)
    grad_scores = jnp.einsum(
        "shj,thj->hst", attention_grad, value_heads, preferred_element_type=jnp.float32
    )
    grad_scores = (grad_scores * causal).astype(jnp.bfloat16)
    local_grad = jnp.einsum(
        "chi,chj->hij", query_heads, attention_grad, preferred_element_type=jnp.float32
    )
    suffix_state = prefix(local_grad, "seq", add_states, jnp.zeros_like(local_grad))
    suffix_rounded = suffix_state.astype(jnp.bfloat16)
    query_grad = jnp.einsum(
        "shj,hij->shi", attention_grad, prefix_rounded, preferred_element_type=jnp.float32
    )
    query_grad = query_grad + jnp.einsum(
        "hst,thi->shi", grad_scores, key_heads, preferred_element_type=jnp.float32
    )
    key_grad = jnp.einsum(
        "thj,hij->thi", value_heads, suffix_rounded, preferred_element_type=jnp.float32
    )
    key_grad = key_grad + jnp.einsum(
        "hst,shi->thi", grad_scores, query_heads, preferred_element_type=jnp.float32
    )
    value_grad = jnp.einsum(
        "thi,hij->thj", key_heads, suffix_rounded, preferred_element_type=jnp.float32
    )
    value_grad = value_grad + jnp.einsum(
        "hst,shj->thj", block_scores, attention_grad, preferred_element_type=jnp.float32
    )

    def finish(tensor):
        return tensor.astype(jnp.bfloat16).reshape(1, positions_count, features)

    return (layer_output, finish(query_grad), finish(key_grad), finish(value_grad))


MESH = pl.DeviceIdType.MESH
F32, BF16 = jnp.float32, jnp.bfloat16
PIECES = ((0, 2), (2, 2), (4, 2), (6, 1), (7, 1))
GROUPS = 4
EARLY = 6
LATE = 3
ORDER = (0, 1, 3, 4, 2)


def dot(a, b, ca, cb):
    return lax.dot_general(a, b, (((ca,), (cb,)), ((), ())), preferred_element_type=F32)


def body(nz, head_count, rows, wd, *refs):
    (q_in, k_in, v_in, w, cot, out, qg, kg, vg, wg, cotg, lst, pin, pout, scores, att, normg, acc, ngs, ngr,
     osend, orecv, oacc, ofin, ag, kloc, vloc, near, far, sout,
     q, k, v, in_sem, own_sem, w_s, w_r, c_s, c_r, r_s, r_r, p_s, p_r, a_s, a_r, b_s, b_r, n_s, n_r, g_s, g_r, o_s, o_r, f_s, f_r) = refs
    z, x = lax.axis_index("seq"), lax.axis_index("dp")
    y, s = lax.axis_index("groups"), lax.axis_index("sub")
    half, hb, feat = wd // 2, nz // 2, head_count * HS
    per = head_count // GROUPS
    last = nz - 1
    peers = (1, 2, 3)

    def place(j):
        return lax.rem(x + (j & 1), 2), lax.rem(y + (j >> 1), 2)

    def to_peer(j):
        xj, yj = place(j)
        return {"dp": xj, "groups": yj}

    def remote(src, dst, send, recv, device):
        return pltpu.make_async_remote_copy(
            src_ref=src, dst_ref=dst, send_sem=send, recv_sem=recv, device_id=device, device_id_type=MESH)

    other = {"sub": 1 - s}

    loads = [pltpu.make_async_copy(a, b, in_sem.at[i]) for i, (a, b) in enumerate(((k_in, k), (v_in, v), (q_in, q)))]
    for load in loads:
        load.start()

    barrier = pltpu.get_barrier_semaphore()
    for j in peers:
        pl.semaphore_signal(barrier, inc=1, device_id=to_peer(j), device_id_type=MESH)
    for d in range(1, nz):
        pl.semaphore_signal(barrier, inc=1, device_id={"seq": lax.rem(z + d, nz)}, device_id_type=MESH)
    pl.semaphore_signal(barrier, inc=1, device_id=other, device_id_type=MESH)
    pl.semaphore_wait(barrier, nz + 3)

    mine = w.at[:, pl.ds(pl.multiple_of(y * half, 128), half)]
    sent = {zz: [] for zz in range(nz)}

    def span(c):
        first, count = PIECES[c]
        return slice(first * HS, (first + count) * HS)

    def w_copy(zz, block, c, dz):
        src = mine if block == zz else wg.at[block]
        return remote(src.at[span(c)], wg.at[block, span(c)], w_s.at[(dz + 1) // 2, block, c], w_r.at[block, c], {"seq": zz + dz})

    def prefix_copy(zz, g):
        part = pl.ds(g * per, per)
        return remote(pout.at[part], pin.at[part], p_s.at[g], p_r.at[g], {"seq": zz + 1})

    def heads_of(c):
        first, count = PIECES[c]
        return pl.ds(first, count)

    def near_copy(zz, c):
        return remote(sout.at[heads_of(c)], near.at[heads_of(c)], a_s.at[c], a_r.at[c], {"seq": zz - 1})

    def far_to(c):
        return range(0 if c >= LATE else 1, last)

    def far_copy(to, c):
        return remote(sout.at[heads_of(c)], far.at[heads_of(c)], b_s.at[to, c], b_r.at[c], {"seq": to})

    def stage(table):
        for zz, ops in table.items():
            @pl.when(z == zz)
            def _():
                for op in ops:
                    if op[0] == "w":
                        copy = w_copy(zz, *op[1:])
                        if op[1] != zz:
                            w_copy(zz, op[1], op[2], op[3]).wait_recv()
                        copy.start()
                        sent[zz].append((w_copy, op[1:]))
                    elif op[0] == "p":
                        g = op[1]
                        part = slice(g * per, (g + 1) * per)
                        copy = prefix_copy(min(zz, last - 1), g)
                        if zz > 0:
                            copy.wait_recv()
                        if zz == 0:
                            pout[part] = lst[part].astype(BF16)
                            pin[part] = jnp.zeros((per, HS, HS), BF16)
                        elif zz < last:
                            pout[part] = (pin[part].astype(F32) + lst[part]).astype(BF16)
                        if zz < last:
                            copy.start()
                            sent[zz].append((prefix_copy, (g,)))

    def own(c, *ways):
        return [("w", None, c, way) for way in ways]

    def table(**rows_of):
        made = {}
        for name, ops in rows_of.items():
            zz = int(name[1:])
            made[zz] = [tuple(zz if (i == 1 and part is None) else part for i, part in enumerate(op)) for op in ops]
        return made

    stage(table(
        z0=own(0, 1),
        z1=own(0, 1, -1) + own(1, 1, -1),
        z2=own(0, 1, -1) + own(1, 1, -1),
        z3=[op for c in range(len(PIECES)) for op in own(c, -1)],
    ))
    own_w = pltpu.make_async_copy(mine, wg.at[z], own_sem.at[nz])
    own_w.start()

    share = pl.ds(pl.multiple_of(s * (rows // 2), rows // 2), rows // 2)

    def cot_piece(j, b, which):
        xj, yj = place(j)
        return cot.at[0, which, pl.ds(pl.multiple_of((b * 2 + xj) * wd + yj * half, 128), half)]

    def cot_own(b):
        return pltpu.make_async_copy(cot_piece(0, b, slice(None)), cotg.at[b, 0], own_sem.at[b])

    def cot_copy(j, b):
        return remote(cot_piece(j, b, share), cotg.at[b, j, share], c_s.at[j, b], c_r.at[j, b], to_peer(j))

    def cot_across(j):
        return remote(cotg.at[:, j, share], cotg.at[:, j, share], r_s.at[j], r_r.at[j], other)

    for b in range(nz):
        cot_own(b).start()
        for j in peers:
            cot_copy(j, b).start()

    def col(h):
        return slice(h * HS, (h + 1) * HS)

    for load in loads:
        load.wait()
    for h in range(head_count):
        lst[h] = dot(k[0, :, col(h)], v[0, :, col(h)], 0, 0)
    stage(table(
        z0=[("p", g) for g in range(GROUPS)] + [op for c in range(1, len(PIECES)) for op in own(c, 1)],
    ))

    @pl.when(z >= 2)
    def _():
        near[...] = jnp.zeros(near.shape, BF16)

    @pl.when(z == last)
    def _():
        far[...] = jnp.zeros(far.shape, BF16)

    @pl.when(z == 0)
    def _():
        for c in range(LATE):
            part = heads_of(c)
            far[part] = jnp.zeros((PIECES[c][1], HS, HS), BF16)

    causal = (lax.broadcasted_iota(jnp.int32, (rows, rows), 1) <= lax.broadcasted_iota(jnp.int32, (rows, rows), 0))
    for h in range(head_count):
        product = dot(q[0, :, col(h)], k[0, :, col(h)], 1, 1)
        scores[h] = jnp.where(causal, product, 0.0).astype(BF16)
    for h in range(head_count):
        att[h] = dot(scores[h], v[0, :, col(h)], 1, 0)

    def normed_copy(j, g):
        part = slice(g * per * HS, (g + 1) * per * HS)
        return remote(normg.at[0, :, part], normg.at[j, :, part], n_s.at[j, g], n_r.at[j, g], to_peer(j))

    def grad_copy(j, c):
        return remote(ngs.at[j, :, span(c)], ngr.at[j, :, span(c)], g_s.at[j, c], g_r.at[j, c], to_peer(j))

    def attend(g):
        for h in range(g * per, (g + 1) * per):
            total = att[h] + dot(q[0, :, col(h)], pin[h], 1, 0)
            att[h] = total
            factor = lax.rsqrt(jnp.mean(total * total, axis=-1, keepdims=True) + 1e-05)
            normg[0, :, col(h)] = (total * factor).astype(BF16)
        for j in peers:
            normed_copy(j, g).start()

    def gradient(c):
        for zz in (0, last):
            @pl.when(z == zz)
            def _():
                for b in range(nz):
                    if b != zz:
                        w_copy(zz, b, c, 1 if zz == 0 else -1).wait_recv()
        part = span(c)
        total = dot(cotg[0].reshape(4 * rows, half), wg[0, part, :], 1, 1)
        for b in range(1, nz):
            total = total + dot(cotg[b].reshape(4 * rows, half), wg[b, part, :], 1, 1)
        acc[:, part] = total[:rows]
        for j in peers:
            ngs[j, :, part] = total[j * rows:(j + 1) * rows].astype(BF16)
            grad_copy(j, c).start()

    def turn(c):
        for j in peers:
            grad_copy(j, c).wait_recv()
        first, count = PIECES[c]
        for h in range(first, first + count):
            grad = acc[:, col(h)]
            for j in peers:
                grad = grad + ngr[j, :, col(h)].astype(F32)
            total = att[h]
            factor = lax.rsqrt(jnp.mean(total * total, axis=-1, keepdims=True) + 1e-05)
            mean_term = jnp.mean(total * grad, axis=-1, keepdims=True)
            turned = (factor * grad - total * (factor * factor * factor) * mean_term).astype(BF16)
            ag[h] = turned
            lst[h] = dot(q[0, :, col(h)], turned, 0, 0)
            sout[h] = lst[h].astype(BF16)

        @pl.when(z == last)
        def _():
            for to in far_to(c):
                far_copy(to, c).start()

        @pl.when(z == 2)
        def _():
            near_copy(2, c).start()

    def finish(c):
        first, count = PIECES[c]
        for h in range(first, first + count):
            turned = ag[h]
            grad_scores = jnp.where(causal, dot(turned, v[0, :, col(h)], 1, 1), 0.0).astype(BF16)
            qg[0, :, col(h)] = (dot(turned, pin[h], 1, 1) + dot(grad_scores, k[0, :, col(h)], 1, 0)).astype(BF16)
            kloc[h] = dot(grad_scores, q[0, :, col(h)], 0, 0)
            vloc[h] = dot(scores[h], turned, 0, 0)

    def up(block, c):
        return ("w", block, c, 1)

    def down(block, c):
        return ("w", block, c, -1)

    stage(table(
        z1=[up(0, 0), down(2, 0)],
        z2=[up(1, 0), down(3, 0)],
    ))
    for g in range(GROUPS):
        stage(table(
            z1=[("p", g)] + ([down(2, 1)] if g == 0 else [down(3, 0)] if g == GROUPS - 1 else []),
            z2=([up(1, 1), down(3, 1), up(0, 0)] + own(2, -1) if g == 0 else []) + [("p", g)],
            z3=[("p", g)],
        ))
        attend(g)
        if g == 0:
            for j in peers:
                for b in range(nz):
                    cot_copy(j, b).wait_recv()
                cot_across(j).start()
    stage(table(
        z1=[up(0, 1), down(3, 1)] + own(2, 1, -1),
        z2=[down(3, 2)] + own(3, -1) + [up(0, 1)] + own(2, 1),
    ))
    own_w.wait()
    for b in range(nz):
        cot_own(b).wait()
    for j in peers:
        cot_across(j).wait_recv()
    gradient(0)
    stage(table(
        z1=[up(0, 2), down(2, 2), down(3, 2)] + own(3, 1, -1),
        z2=[down(3, 3), up(1, 2), up(0, 2)] + own(3, 1),
    ))
    gradient(1)
    stage(table(
        z1=[up(0, 3), down(2, 3), down(3, 3)] + own(4, 1, -1) + [up(0, 4), down(2, 4), down(3, 4)],
        z2=own(4, -1) + [down(3, 4), up(1, 3), up(0, 3)] + own(4, 1) + [up(1, 4), up(0, 4)],
    ))
    gradient(2)
    turn(0)
    for j in peers:
        for g in range(GROUPS):
            normed_copy(j, g).wait_recv()
    deep = EARLY * HS

    @pl.loop(0, nz)
    def _(b):
        left = normg[:, :, :deep].reshape(4 * rows, deep)
        oacc[b] = dot(left, wg[b, :deep], 1, 0).reshape(4, rows, half)

    finish(0)
    gradient(3)
    turn(1)
    finish(1)
    turn(2)
    finish(2)
    gradient(4)

    def sub_copy(i):
        return remote(osend.at[i], orecv.at[i], o_s.at[i], o_r.at[i], other)

    left = normg[:, :, deep:].reshape(4 * rows, feat - deep)
    for i in range(hb):
        there = (1 - s) * hb + i
        osend[i] = (oacc[there] + dot(left, wg[there, deep:], 1, 0).reshape(4, rows, half)).astype(BF16)
        sub_copy(i).start()
    for i in range(hb):
        here = s * hb + i
        oacc[here] = oacc[here] + dot(left, wg[here, deep:], 1, 0).reshape(4, rows, half)
    turn(3)

    def out_part(i, xj, yj):
        return out.at[0, :, pl.ds(pl.multiple_of((i * 2 + xj) * wd + yj * half, 128), half)]

    def out_copy(i, j):
        return remote(ofin.at[i, j], out_part(i, x, y), f_s.at[i, j], f_r.at[i, j], to_peer(j))

    for i in range(hb):
        sub_copy(i).wait_recv()
        ofin[i] = (oacc[s * hb + i] + orecv[i].astype(F32)).astype(BF16)
        for j in peers:
            out_copy(i, j).start()
        out_part(i, x, y)[...] = ofin[i, 0]

    turn(4)

    @pl.when(z == 1)
    def _():
        for c in ORDER:
            near_copy(1, c).wait_recv()
            part = heads_of(c)
            added = near[part].astype(F32) + lst[part]
            if c < LATE:
                far_copy(1, c).wait_recv()
                added = added + far[part].astype(F32)
            sout[part] = added.astype(BF16)
            near_copy(1, c).start()

    finish(3)
    finish(4)
    for zz in range(nz):
        @pl.when(z == zz)
        def _():
            for make, where in sent[zz]:
                make(zz, *where).wait_send()
    for j in peers:
        for b in range(nz):
            cot_copy(j, b).wait_send()
        cot_across(j).wait_send()
        for g in range(GROUPS):
            normed_copy(j, g).wait_send()
        for c in range(len(PIECES)):
            grad_copy(j, c).wait_send()
    for i in range(hb):
        sub_copy(i).wait_send()

    for c in range(len(PIECES)):
        @pl.when(z == 0)
        def _():
            near_copy(1, c).wait_recv()

        if c < LATE:
            @pl.when(z == 2)
            def _():
                far_copy(2, c).wait_recv()
        else:
            @pl.when(z < last)
            def _():
                far_copy(0, c).wait_recv()
        first, count = PIECES[c]
        for h in range(first, first + count):
            carried = (near[h].astype(F32) + far[h].astype(F32)).astype(BF16)
            kg[0, :, col(h)] = (kloc[h] + dot(v[0, :, col(h)], carried, 1, 1)).astype(BF16)
            vg[0, :, col(h)] = (vloc[h] + dot(k[0, :, col(h)], carried, 1, 0)).astype(BF16)

    for i in range(hb):
        for j in peers:
            out_copy(i, j).wait_recv()

    for zz in range(nz):
        @pl.when(z == zz)
        def _():
            for c in range(len(PIECES)):
                if zz == last:
                    for to in far_to(c):
                        far_copy(to, c).wait_send()
                elif zz > 0:
                    near_copy(zz, c).wait_send()
    for j in peers:
        for i in range(hb):
            out_copy(i, j).wait_send()


def hand_over(*refs):
    copies = [pltpu.make_async_copy(refs[i], refs[4 + i], refs[8].at[i]) for i in range(4)]
    for copy in copies:
        copy.start()
    for copy in copies:
        copy.wait()


def fused(nz, queries, key_vectors, value_vectors, out_weight, out_cotangent):
    rows, feat = queries.shape[1:]
    wd = out_weight.shape[1]
    heads, half, hb, pieces = feat // HS, wd // 2, nz // 2, len(PIECES)
    vmem, dma = pltpu.VMEM, pltpu.SemaphoreType.DMA
    states = (heads, HS, HS)
    inside = pl.BlockSpec(memory_space=pltpu.VMEM)
    outside = pl.BlockSpec(memory_space=pltpu.HBM)
    grads = pltpu.VMEM((1, rows, feat), BF16)
    outs = pl.pallas_call(
        functools.partial(body, nz, heads, rows, wd),
        out_shape=(pltpu.VMEM((1, rows, nz * wd), BF16), grads, grads, grads),
        in_specs=[outside] * 5,
        out_specs=(inside,) * 4,
        scratch_shapes=[
            vmem((nz, feat, half), BF16), vmem((nz, 4, rows, half), BF16),
            vmem(states, F32), vmem(states, BF16), vmem(states, BF16),
            vmem((heads, rows, rows), BF16), vmem((heads, rows, HS), F32),
            vmem((4, rows, feat), BF16), vmem((rows, feat), F32),
            vmem((4, rows, feat), BF16), vmem((4, rows, feat), BF16),
            vmem((hb, 4, rows, half), BF16), vmem((hb, 4, rows, half), BF16),
            vmem((nz, 4, rows, half), F32), vmem((hb, 4, rows, half), BF16),
            vmem((heads, rows, HS), BF16), vmem((heads, rows, HS), F32), vmem((heads, rows, HS), F32),
            vmem(states, BF16), vmem(states, BF16), vmem(states, BF16),
            vmem((1, rows, feat), BF16), vmem((1, rows, feat), BF16), vmem((1, rows, feat), BF16), dma((3,)),
            dma((nz + 1,)), dma((2, nz, pieces)), dma((nz, pieces)),
            dma((4, nz)), dma((4, nz)), dma((4,)), dma((4,)), dma((GROUPS,)), dma((GROUPS,)),
            dma((pieces,)), dma((pieces,)), dma((nz, pieces)), dma((pieces,)),
            dma((4, GROUPS)), dma((4, GROUPS)), dma((4, pieces)), dma((4, pieces)),
            dma((hb,)), dma((hb,)), dma((hb, 4)), dma((hb, 4)),
        ],
        compiler_params=pltpu.CompilerParams(
            collective_id=0, has_side_effects=True, vmem_limit_bytes=60 * 1024 * 1024),
    )(queries, key_vectors, value_vectors, out_weight, out_cotangent)
    grads = jax.ShapeDtypeStruct((1, rows, feat), BF16)
    return tuple(pl.pallas_call(
        hand_over,
        out_shape=(jax.ShapeDtypeStruct((1, rows, nz * wd), BF16), grads, grads, grads),
        in_specs=[pl.BlockSpec(memory_space=pltpu.VMEM)] * 4,
        out_specs=(outside,) * 4,
        scratch_shapes=[dma((4,))],
    )(*(pltpu.with_memory_space_constraint(o, pltpu.VMEM) for o in outs)))


def solution(mesh):
    placed = (
        P(("groups", "dp"), "seq", "sub"),
        P(("groups", "dp"), "seq", "sub"),
        P(("groups", "dp"), "seq", "sub"),
        P("sub", ("seq", "dp")),
        P(("groups", "dp"), "seq", None),
    )
    shape = dict(mesh.shape)
    count = shape["seq"]

    def part(queries, key_vectors, value_vectors, out_weight, out_cotangent):
        args = (queries, key_vectors, value_vectors, out_weight, out_cotangent)
        fits = shape["groups"] == shape["dp"] == shape["sub"] == 2 and count == 4
        if fits and queries.shape[2] == 8 * HS and out_weight.shape[1] % 256 == 0:
            return fused(count, *args)
        return local(*args)

    return jax.shard_map(
        part,
        mesh=mesh,
        in_specs=placed,
        out_specs=(
            P(("groups", "dp"), "seq", "sub"),
            P(("groups", "dp"), "seq", "sub"),
            P(("groups", "dp"), "seq", "sub"),
            P(("groups", "dp"), "seq", "sub"),
        ),
        check_vma=False,
    )
```

```python
import functools

import jax
import jax.numpy as jnp
from jax import lax
from jax.experimental import pallas as pl
from jax.experimental.pallas import tpu as pltpu
from jax.sharding import PartitionSpec as P

HS = 128


def carried_in(value, axis, join, neutral):
    count, mine = (lax.axis_size(axis), lax.axis_index(axis))
    pieces = lax.all_gather(value, axis)
    total = jnp.full_like(value, 0) + jnp.asarray(neutral, value.dtype)

    def step(position, total):
        longer = join(total, pieces[position])
        return jnp.where(position < mine, longer, total)

    return lax.fori_loop(0, count - 1, step, total)


def prefix(shard, axis, join, neutral):
    count = lax.axis_size(axis)
    place = lax.axis_index(axis)
    ahead = count - 1 - place
    gathered = lax.all_gather(shard.astype(jnp.bfloat16), axis)
    state = jnp.zeros_like(shard) + jnp.asarray(neutral, shard.dtype)

    def one(step, state):
        source = count - 1 - step
        return join(state, lax.dynamic_index_in_dim(gathered, source, 0, False).astype(shard.dtype))

    return lax.fori_loop(0, ahead, one, state)


def add_states(earlier, later):
    return earlier + later


def rms_factor(attention):
    return lax.rsqrt(jnp.mean(attention * attention, axis=-1, keepdims=True) + 1e-05)


def causal_mask(positions_count):
    positions = lax.broadcasted_iota(jnp.int32, (positions_count, positions_count), 0)
    columns = lax.broadcasted_iota(jnp.int32, (positions_count, positions_count), 1)
    return (columns <= positions).astype(jnp.float32)


def local(queries, key_vectors, value_vectors, out_weight, out_cotangent):
    positions_count = queries.shape[1]
    features = queries.shape[2]
    head_count = features // HS
    query_heads = queries[0].reshape(positions_count, head_count, HS)
    key_heads = key_vectors[0].reshape(positions_count, head_count, HS)
    value_heads = value_vectors[0].reshape(positions_count, head_count, HS)
    causal = causal_mask(positions_count)
    local_state = jnp.einsum(
        "chi,chj->hij", key_heads, value_heads, preferred_element_type=jnp.float32
    )
    prefix_state = carried_in(local_state, "seq", add_states, jnp.zeros_like(local_state))
    prefix_rounded = prefix_state.astype(jnp.bfloat16)
    block_scores = jnp.einsum(
        "shi,thi->hst", query_heads, key_heads, preferred_element_type=jnp.float32
    )
    block_scores = (block_scores * causal).astype(jnp.bfloat16)
    attention = jnp.einsum(
        "shi,hij->shj", query_heads, prefix_rounded, preferred_element_type=jnp.float32
    )
    attention = attention + jnp.einsum(
        "hst,thj->shj", block_scores, value_heads, preferred_element_type=jnp.float32
    )
    factor = rms_factor(attention)
    normed = (attention * factor).astype(jnp.bfloat16).reshape(positions_count, features)
    cotangent = out_cotangent[0]
    weight_piece = lax.all_gather(out_weight, ("seq", "dp"), axis=1, tiled=True)
    product = jnp.dot(normed, weight_piece, preferred_element_type=jnp.float32)
    output_part = product
    normed_grad = lax.dot_general(
        cotangent, weight_piece, (((1,), (1,)), ((), ())), preferred_element_type=jnp.float32
    )
    output_part, normed_grad = (output_part, normed_grad)
    layer_output = lax.psum_scatter(
        output_part.astype(jnp.bfloat16), "sub", scatter_dimension=1, tiled=True
    )[None]
    grad_heads = normed_grad.reshape(positions_count, head_count, HS)
    mean_term = jnp.mean(attention * grad_heads, axis=-1, keepdims=True)
    attention_grad = (
        factor * grad_heads - attention * (factor * factor * factor) * mean_term
    ).astype(jnp.bfloat16)
    grad_scores = jnp.einsum(
        "shj,thj->hst", attention_grad, value_heads, preferred_element_type=jnp.float32
    )
    grad_scores = (grad_scores * causal).astype(jnp.bfloat16)
    local_grad = jnp.einsum(
        "chi,chj->hij", query_heads, attention_grad, preferred_element_type=jnp.float32
    )
    suffix_state = prefix(local_grad, "seq", add_states, jnp.zeros_like(local_grad))
    suffix_rounded = suffix_state.astype(jnp.bfloat16)
    query_grad = jnp.einsum(
        "shj,hij->shi", attention_grad, prefix_rounded, preferred_element_type=jnp.float32
    )
    query_grad = query_grad + jnp.einsum(
        "hst,thi->shi", grad_scores, key_heads, preferred_element_type=jnp.float32
    )
    key_grad = jnp.einsum(
        "thj,hij->thi", value_heads, suffix_rounded, preferred_element_type=jnp.float32
    )
    key_grad = key_grad + jnp.einsum(
        "hst,shi->thi", grad_scores, query_heads, preferred_element_type=jnp.float32
    )
    value_grad = jnp.einsum(
        "thi,hij->thj", key_heads, suffix_rounded, preferred_element_type=jnp.float32
    )
    value_grad = value_grad + jnp.einsum(
        "hst,shj->thj", block_scores, attention_grad, preferred_element_type=jnp.float32
    )

    def finish(tensor):
        return tensor.astype(jnp.bfloat16).reshape(1, positions_count, features)

    return (layer_output, finish(query_grad), finish(key_grad), finish(value_grad))


MESH = pl.DeviceIdType.MESH
F32, BF16 = jnp.float32, jnp.bfloat16
PIECES = ((0, 2), (2, 2), (4, 2), (6, 1), (7, 1))
GROUPS = 4
EARLY = 6
LATE = 3
ORDER = (0, 1, 3, 4, 2)


def dot(a, b, ca, cb):
    return lax.dot_general(a, b, (((ca,), (cb,)), ((), ())), preferred_element_type=F32)


def body(nz, head_count, rows, wd, *refs):
    (q_in, k_in, v_in, w, cot, out, qg, kg, vg, wg, cotg, lst, pin, pout, scores, att, normg, acc, ngs, ngr,
     osend, orecv, oacc, ofin, ag, kloc, vloc, near, far, sout,
     q, k, v, in_sem, own_sem, w_s, w_r, c_s, c_r, r_s, r_r, p_s, p_r, a_s, a_r, b_s, b_r, n_s, n_r, g_s, g_r, o_s, o_r, f_s, f_r) = refs
    z, x = lax.axis_index("seq"), lax.axis_index("dp")
    y, s = lax.axis_index("groups"), lax.axis_index("sub")
    half, hb, feat = wd // 2, nz // 2, head_count * HS
    per = head_count // GROUPS
    last = nz - 1
    peers = (3, 1, 2)

    def place(j):
        return lax.rem(x + (j & 1), 2), lax.rem(y + (j >> 1), 2)

    def to_peer(j):
        xj, yj = place(j)
        return {"dp": xj, "groups": yj}

    def remote(src, dst, send, recv, device):
        return pltpu.make_async_remote_copy(
            src_ref=src, dst_ref=dst, send_sem=send, recv_sem=recv, device_id=device, device_id_type=MESH)

    other = {"sub": 1 - s}

    loads = [pltpu.make_async_copy(a, b, in_sem.at[i]) for i, (a, b) in enumerate(((k_in, k), (v_in, v), (q_in, q)))]
    barrier = pltpu.get_barrier_semaphore()
    for j in peers:
        pl.semaphore_signal(barrier, inc=1, device_id=to_peer(j), device_id_type=MESH)
    for d in range(1, nz):
        pl.semaphore_signal(barrier, inc=1, device_id={"seq": lax.rem(z + d, nz)}, device_id_type=MESH)
    pl.semaphore_signal(barrier, inc=1, device_id=other, device_id_type=MESH)
    for load in loads:
        load.start()
    pl.semaphore_wait(barrier, nz + 3)

    mine = w.at[:, pl.ds(pl.multiple_of(y * half, 128), half)]
    sent = {zz: [] for zz in range(nz)}

    def span(c):
        first, count = PIECES[c]
        return slice(first * HS, (first + count) * HS)

    def w_copy(zz, block, c, dz):
        src = mine if block == zz else wg.at[block]
        return remote(src.at[span(c)], wg.at[block, span(c)], w_s.at[(dz + 1) // 2, block, c], w_r.at[block, c], {"seq": zz + dz})

    def prefix_copy(zz, g):
        part = pl.ds(g * per, per)
        return remote(pout.at[part], pin.at[part], p_s.at[g], p_r.at[g], {"seq": zz + 1})

    def heads_of(c):
        first, count = PIECES[c]
        return pl.ds(first, count)

    def near_copy(zz, c):
        return remote(sout.at[heads_of(c)], near.at[heads_of(c)], a_s.at[c], a_r.at[c], {"seq": zz - 1})

    def far_to(c):
        return range(0 if c >= LATE else 1, last)

    def far_copy(to, c):
        return remote(sout.at[heads_of(c)], far.at[heads_of(c)], b_s.at[to, c], b_r.at[c], {"seq": to})

    def stage(table):
        for zz, ops in table.items():
            @pl.when(z == zz)
            def _():
                for op in ops:
                    if op[0] == "w":
                        copy = w_copy(zz, *op[1:])
                        if op[1] != zz:
                            w_copy(zz, op[1], op[2], op[3]).wait_recv()
                        copy.start()
                        sent[zz].append((w_copy, op[1:]))
                    elif op[0] == "p":
                        g = op[1]
                        part = slice(g * per, (g + 1) * per)
                        copy = prefix_copy(min(zz, last - 1), g)
                        if zz > 0:
                            copy.wait_recv()
                        if zz == 0:
                            pout[part] = lst[part].astype(BF16)
                            pin[part] = jnp.zeros((per, HS, HS), BF16)
                        elif zz < last:
                            pout[part] = (pin[part].astype(F32) + lst[part]).astype(BF16)
                        if zz < last:
                            copy.start()
                            sent[zz].append((prefix_copy, (g,)))

    def own(c, *ways):
        return [("w", None, c, way) for way in ways]

    def table(**rows_of):
        made = {}
        for name, ops in rows_of.items():
            zz = int(name[1:])
            made[zz] = [tuple(zz if (i == 1 and part is None) else part for i, part in enumerate(op)) for op in ops]
        return made

    stage(table(
        z0=own(0, 1),
        z1=own(0, 1, -1) + own(1, 1, -1),
        z2=own(0, 1, -1) + own(1, 1, -1),
        z3=[op for c in range(len(PIECES)) for op in own(c, -1)],
    ))
    own_w = pltpu.make_async_copy(mine, wg.at[z], own_sem.at[nz])
    own_w.start()

    share = pl.ds(pl.multiple_of(s * (rows // 2), rows // 2), rows // 2)

    def cot_piece(j, b, which):
        xj, yj = place(j)
        return cot.at[0, which, pl.ds(pl.multiple_of((b * 2 + xj) * wd + yj * half, 128), half)]

    def cot_own(b):
        return pltpu.make_async_copy(cot_piece(0, b, slice(None)), cotg.at[b, 0], own_sem.at[b])

    def cot_copy(j, b):
        return remote(cot_piece(j, b, share), cotg.at[b, j, share], c_s.at[j, b], c_r.at[j, b], to_peer(j))

    def cot_across(j):
        return remote(cotg.at[:, j, share], cotg.at[:, j, share], r_s.at[j], r_r.at[j], other)

    for b in range(nz):
        cot_own(b).start()
        for j in peers:
            cot_copy(j, b).start()

    def col(h):
        return slice(h * HS, (h + 1) * HS)

    for load in loads:
        load.wait()
    for h in range(head_count):
        lst[h] = dot(k[0, :, col(h)], v[0, :, col(h)], 0, 0)
    stage(table(
        z0=[("p", g) for g in range(GROUPS)] + [op for c in range(1, len(PIECES)) for op in own(c, 1)],
    ))

    @pl.when(z >= 2)
    def _():
        near[...] = jnp.zeros(near.shape, BF16)

    @pl.when(z == last)
    def _():
        far[...] = jnp.zeros(far.shape, BF16)

    @pl.when(z == 0)
    def _():
        for c in range(LATE):
            part = heads_of(c)
            far[part] = jnp.zeros((PIECES[c][1], HS, HS), BF16)

    causal = (lax.broadcasted_iota(jnp.int32, (rows, rows), 1) <= lax.broadcasted_iota(jnp.int32, (rows, rows), 0))
    for h in range(head_count):
        product = dot(q[0, :, col(h)], k[0, :, col(h)], 1, 1)
        scores[h] = jnp.where(causal, product, 0.0).astype(BF16)
    for h in range(head_count):
        att[h] = dot(scores[h], v[0, :, col(h)], 1, 0)

    def normed_copy(j, g):
        part = slice(g * per * HS, (g + 1) * per * HS)
        return remote(normg.at[0, :, part], normg.at[j, :, part], n_s.at[j, g], n_r.at[j, g], to_peer(j))

    def grad_copy(j, c):
        return remote(ngs.at[j, :, span(c)], ngr.at[j, :, span(c)], g_s.at[j, c], g_r.at[j, c], to_peer(j))

    def attend(g):
        for h in range(g * per, (g + 1) * per):
            total = att[h] + dot(q[0, :, col(h)], pin[h], 1, 0)
            att[h] = total
            factor = lax.rsqrt(jnp.mean(total * total, axis=-1, keepdims=True) + 1e-05)
            normg[0, :, col(h)] = (total * factor).astype(BF16)
        for j in peers:
            normed_copy(j, g).start()

    def gradient(c):
        for zz in (0, last):
            @pl.when(z == zz)
            def _():
                for b in range(nz):
                    if b != zz:
                        w_copy(zz, b, c, 1 if zz == 0 else -1).wait_recv()
        part = span(c)
        total = dot(cotg[0].reshape(4 * rows, half), wg[0, part, :], 1, 1)
        for b in range(1, nz):
            total = total + dot(cotg[b].reshape(4 * rows, half), wg[b, part, :], 1, 1)
        acc[:, part] = total[:rows]
        for j in peers:
            ngs[j, :, part] = total[j * rows:(j + 1) * rows].astype(BF16)
            grad_copy(j, c).start()

    def turn(c):
        for j in peers:
            grad_copy(j, c).wait_recv()
        first, count = PIECES[c]
        for h in range(first, first + count):
            grad = acc[:, col(h)]
            for j in peers:
                grad = grad + ngr[j, :, col(h)].astype(F32)
            total = att[h]
            factor = lax.rsqrt(jnp.mean(total * total, axis=-1, keepdims=True) + 1e-05)
            mean_term = jnp.mean(total * grad, axis=-1, keepdims=True)
            turned = (factor * grad - total * (factor * factor * factor) * mean_term).astype(BF16)
            ag[h] = turned
            lst[h] = dot(q[0, :, col(h)], turned, 0, 0)
            sout[h] = lst[h].astype(BF16)

        @pl.when(z == last)
        def _():
            for to in far_to(c):
                far_copy(to, c).start()

        @pl.when(z == 2)
        def _():
            near_copy(2, c).start()

    def finish(c):
        first, count = PIECES[c]
        for h in range(first, first + count):
            turned = ag[h]
            grad_scores = jnp.where(causal, dot(turned, v[0, :, col(h)], 1, 1), 0.0).astype(BF16)
            qg[0, :, col(h)] = (dot(turned, pin[h], 1, 1) + dot(grad_scores, k[0, :, col(h)], 1, 0)).astype(BF16)
            kloc[h] = dot(grad_scores, q[0, :, col(h)], 0, 0)
            vloc[h] = dot(scores[h], turned, 0, 0)

    def up(block, c):
        return ("w", block, c, 1)

    def down(block, c):
        return ("w", block, c, -1)

    stage(table(
        z1=[up(0, 0), down(2, 0)],
        z2=[up(1, 0), down(3, 0)],
    ))
    for g in range(GROUPS):
        stage(table(
            z1=[("p", g)] + ([down(2, 1)] if g == 0 else [down(3, 0)] if g == GROUPS - 1 else []),
            z2=([up(1, 1), down(3, 1), up(0, 0)] + own(2, -1) if g == 0 else []) + [("p", g)],
            z3=[("p", g)],
        ))
        attend(g)
        if g == 0:
            for j in peers:
                for b in range(nz):
                    cot_copy(j, b).wait_recv()
                cot_across(j).start()
    stage(table(
        z1=[up(0, 1), down(3, 1)] + own(2, 1, -1),
        z2=[down(3, 2)] + own(3, -1) + [up(0, 1)] + own(2, 1),
    ))
    own_w.wait()
    for b in range(nz):
        cot_own(b).wait()
    for j in peers:
        cot_across(j).wait_recv()
    gradient(0)
    stage(table(
        z1=[up(0, 2), down(2, 2), down(3, 2)] + own(3, 1, -1),
        z2=[down(3, 3), up(1, 2), up(0, 2)] + own(3, 1),
    ))
    gradient(1)
    stage(table(
        z1=[up(0, 3), down(2, 3), down(3, 3)] + own(4, 1, -1) + [up(0, 4), down(2, 4), down(3, 4)],
        z2=own(4, -1) + [down(3, 4), up(1, 3), up(0, 3)] + own(4, 1) + [up(1, 4), up(0, 4)],
    ))
    gradient(2)
    turn(0)
    for j in peers:
        for g in range(GROUPS):
            normed_copy(j, g).wait_recv()
    deep = EARLY * HS

    @pl.loop(0, nz)
    def _(b):
        left = normg[:, :, :deep].reshape(4 * rows, deep)
        oacc[b] = dot(left, wg[b, :deep], 1, 0).reshape(4, rows, half)

    finish(0)
    gradient(3)
    turn(1)
    finish(1)
    turn(2)
    finish(2)
    gradient(4)

    def sub_copy(i):
        return remote(osend.at[i], orecv.at[i], o_s.at[i], o_r.at[i], other)

    left = normg[:, :, deep:].reshape(4 * rows, feat - deep)
    for i in range(hb):
        there = (1 - s) * hb + i
        osend[i] = (oacc[there] + dot(left, wg[there, deep:], 1, 0).reshape(4, rows, half)).astype(BF16)
        sub_copy(i).start()
    for i in range(hb):
        here = s * hb + i
        oacc[here] = oacc[here] + dot(left, wg[here, deep:], 1, 0).reshape(4, rows, half)
    turn(3)

    def out_part(i, xj, yj):
        return out.at[0, :, pl.ds(pl.multiple_of((i * 2 + xj) * wd + yj * half, 128), half)]

    def out_copy(i, j):
        return remote(ofin.at[i, j], out_part(i, x, y), f_s.at[i, j], f_r.at[i, j], to_peer(j))

    for i in range(hb):
        sub_copy(i).wait_recv()
        ofin[i] = (oacc[s * hb + i] + orecv[i].astype(F32)).astype(BF16)
        for j in peers:
            out_copy(i, j).start()
        out_part(i, x, y)[...] = ofin[i, 0]

    turn(4)

    @pl.when(z == 1)
    def _():
        for c in ORDER:
            near_copy(1, c).wait_recv()
            part = heads_of(c)
            added = near[part].astype(F32) + lst[part]
            if c < LATE:
                far_copy(1, c).wait_recv()
                added = added + far[part].astype(F32)
            sout[part] = added.astype(BF16)
            near_copy(1, c).start()

    finish(3)
    finish(4)
    for zz in range(nz):
        @pl.when(z == zz)
        def _():
            for make, where in sent[zz]:
                make(zz, *where).wait_send()
    for j in peers:
        for b in range(nz):
            cot_copy(j, b).wait_send()
        cot_across(j).wait_send()
        for g in range(GROUPS):
            normed_copy(j, g).wait_send()
        for c in range(len(PIECES)):
            grad_copy(j, c).wait_send()
    for i in range(hb):
        sub_copy(i).wait_send()

    for c in range(len(PIECES)):
        @pl.when(z == 0)
        def _():
            near_copy(1, c).wait_recv()

        if c < LATE:
            @pl.when(z == 2)
            def _():
                far_copy(2, c).wait_recv()
        else:
            @pl.when(z < last)
            def _():
                far_copy(0, c).wait_recv()
        first, count = PIECES[c]
        for h in range(first, first + count):
            carried = (near[h].astype(F32) + far[h].astype(F32)).astype(BF16)
            kg[0, :, col(h)] = (kloc[h] + dot(v[0, :, col(h)], carried, 1, 1)).astype(BF16)
            vg[0, :, col(h)] = (vloc[h] + dot(k[0, :, col(h)], carried, 1, 0)).astype(BF16)

    for i in range(hb):
        for j in peers:
            out_copy(i, j).wait_recv()

    for zz in range(nz):
        @pl.when(z == zz)
        def _():
            for c in range(len(PIECES)):
                if zz == last:
                    for to in far_to(c):
                        far_copy(to, c).wait_send()
                elif zz > 0:
                    near_copy(zz, c).wait_send()
    for j in peers:
        for i in range(hb):
            out_copy(i, j).wait_send()


def hand_over(*refs):
    copies = [pltpu.make_async_copy(refs[i], refs[4 + i], refs[8].at[i]) for i in range(4)]
    for copy in copies:
        copy.start()
    for copy in copies:
        copy.wait()


def fused(nz, queries, key_vectors, value_vectors, out_weight, out_cotangent):
    rows, feat = queries.shape[1:]
    wd = out_weight.shape[1]
    heads, half, hb, pieces = feat // HS, wd // 2, nz // 2, len(PIECES)
    vmem, dma = pltpu.VMEM, pltpu.SemaphoreType.DMA
    states = (heads, HS, HS)
    inside = pl.BlockSpec(memory_space=pltpu.VMEM)
    outside = pl.BlockSpec(memory_space=pltpu.HBM)
    grads = pltpu.VMEM((1, rows, feat), BF16)
    outs = pl.pallas_call(
        functools.partial(body, nz, heads, rows, wd),
        out_shape=(pltpu.VMEM((1, rows, nz * wd), BF16), grads, grads, grads),
        in_specs=[outside] * 5,
        out_specs=(inside,) * 4,
        scratch_shapes=[
            vmem((nz, feat, half), BF16), vmem((nz, 4, rows, half), BF16),
            vmem(states, F32), vmem(states, BF16), vmem(states, BF16),
            vmem((heads, rows, rows), BF16), vmem((heads, rows, HS), F32),
            vmem((4, rows, feat), BF16), vmem((rows, feat), F32),
            vmem((4, rows, feat), BF16), vmem((4, rows, feat), BF16),
            vmem((hb, 4, rows, half), BF16), vmem((hb, 4, rows, half), BF16),
            vmem((nz, 4, rows, half), F32), vmem((hb, 4, rows, half), BF16),
            vmem((heads, rows, HS), BF16), vmem((heads, rows, HS), F32), vmem((heads, rows, HS), F32),
            vmem(states, BF16), vmem(states, BF16), vmem(states, BF16),
            vmem((1, rows, feat), BF16), vmem((1, rows, feat), BF16), vmem((1, rows, feat), BF16), dma((3,)),
            dma((nz + 1,)), dma((2, nz, pieces)), dma((nz, pieces)),
            dma((4, nz)), dma((4, nz)), dma((4,)), dma((4,)), dma((GROUPS,)), dma((GROUPS,)),
            dma((pieces,)), dma((pieces,)), dma((nz, pieces)), dma((pieces,)),
            dma((4, GROUPS)), dma((4, GROUPS)), dma((4, pieces)), dma((4, pieces)),
            dma((hb,)), dma((hb,)), dma((hb, 4)), dma((hb, 4)),
        ],
        compiler_params=pltpu.CompilerParams(
            collective_id=0, has_side_effects=True, vmem_limit_bytes=60 * 1024 * 1024),
    )(queries, key_vectors, value_vectors, out_weight, out_cotangent)
    grads = jax.ShapeDtypeStruct((1, rows, feat), BF16)
    return tuple(pl.pallas_call(
        hand_over,
        out_shape=(jax.ShapeDtypeStruct((1, rows, nz * wd), BF16), grads, grads, grads),
        in_specs=[pl.BlockSpec(memory_space=pltpu.VMEM)] * 4,
        out_specs=(outside,) * 4,
        scratch_shapes=[dma((4,))],
    )(*(pltpu.with_memory_space_constraint(o, pltpu.VMEM) for o in outs)))


def solution(mesh):
    placed = (
        P(("groups", "dp"), "seq", "sub"),
        P(("groups", "dp"), "seq", "sub"),
        P(("groups", "dp"), "seq", "sub"),
        P("sub", ("seq", "dp")),
        P(("groups", "dp"), "seq", None),
    )
    shape = dict(mesh.shape)
    count = shape["seq"]

    def part(queries, key_vectors, value_vectors, out_weight, out_cotangent):
        args = (queries, key_vectors, value_vectors, out_weight, out_cotangent)
        fits = shape["groups"] == shape["dp"] == shape["sub"] == 2 and count == 4
        if fits and queries.shape[2] == 8 * HS and out_weight.shape[1] % 256 == 0:
            return fused(count, *args)
        return local(*args)

    return jax.shard_map(
        part,
        mesh=mesh,
        in_specs=placed,
        out_specs=(
            P(("groups", "dp"), "seq", "sub"),
            P(("groups", "dp"), "seq", "sub"),
            P(("groups", "dp"), "seq", "sub"),
            P(("groups", "dp"), "seq", "sub"),
        ),
        check_vma=False,
    )
```

```python
import functools

import jax
import jax.numpy as jnp
from jax import lax
from jax.experimental import pallas as pl
from jax.experimental.pallas import tpu as pltpu
from jax.sharding import PartitionSpec as P

HS = 128


def carried_in(value, axis, join, neutral):
    count, mine = (lax.axis_size(axis), lax.axis_index(axis))
    pieces = lax.all_gather(value, axis)
    total = jnp.full_like(value, 0) + jnp.asarray(neutral, value.dtype)

    def step(position, total):
        longer = join(total, pieces[position])
        return jnp.where(position < mine, longer, total)

    return lax.fori_loop(0, count - 1, step, total)


def prefix(shard, axis, join, neutral):
    count = lax.axis_size(axis)
    place = lax.axis_index(axis)
    ahead = count - 1 - place
    gathered = lax.all_gather(shard.astype(jnp.bfloat16), axis)
    state = jnp.zeros_like(shard) + jnp.asarray(neutral, shard.dtype)

    def one(step, state):
        source = count - 1 - step
        return join(state, lax.dynamic_index_in_dim(gathered, source, 0, False).astype(shard.dtype))

    return lax.fori_loop(0, ahead, one, state)


def add_states(earlier, later):
    return earlier + later


def rms_factor(attention):
    return lax.rsqrt(jnp.mean(attention * attention, axis=-1, keepdims=True) + 1e-05)


def causal_mask(positions_count):
    positions = lax.broadcasted_iota(jnp.int32, (positions_count, positions_count), 0)
    columns = lax.broadcasted_iota(jnp.int32, (positions_count, positions_count), 1)
    return (columns <= positions).astype(jnp.float32)


def local(queries, key_vectors, value_vectors, out_weight, out_cotangent):
    positions_count = queries.shape[1]
    features = queries.shape[2]
    head_count = features // HS
    query_heads = queries[0].reshape(positions_count, head_count, HS)
    key_heads = key_vectors[0].reshape(positions_count, head_count, HS)
    value_heads = value_vectors[0].reshape(positions_count, head_count, HS)
    causal = causal_mask(positions_count)
    local_state = jnp.einsum(
        "chi,chj->hij", key_heads, value_heads, preferred_element_type=jnp.float32
    )
    prefix_state = carried_in(local_state, "seq", add_states, jnp.zeros_like(local_state))
    prefix_rounded = prefix_state.astype(jnp.bfloat16)
    block_scores = jnp.einsum(
        "shi,thi->hst", query_heads, key_heads, preferred_element_type=jnp.float32
    )
    block_scores = (block_scores * causal).astype(jnp.bfloat16)
    attention = jnp.einsum(
        "shi,hij->shj", query_heads, prefix_rounded, preferred_element_type=jnp.float32
    )
    attention = attention + jnp.einsum(
        "hst,thj->shj", block_scores, value_heads, preferred_element_type=jnp.float32
    )
    factor = rms_factor(attention)
    normed = (attention * factor).astype(jnp.bfloat16).reshape(positions_count, features)
    cotangent = out_cotangent[0]
    weight_piece = lax.all_gather(out_weight, ("seq", "dp"), axis=1, tiled=True)
    product = jnp.dot(normed, weight_piece, preferred_element_type=jnp.float32)
    output_part = product
    normed_grad = lax.dot_general(
        cotangent, weight_piece, (((1,), (1,)), ((), ())), preferred_element_type=jnp.float32
    )
    output_part, normed_grad = (output_part, normed_grad)
    layer_output = lax.psum_scatter(
        output_part.astype(jnp.bfloat16), "sub", scatter_dimension=1, tiled=True
    )[None]
    grad_heads = normed_grad.reshape(positions_count, head_count, HS)
    mean_term = jnp.mean(attention * grad_heads, axis=-1, keepdims=True)
    attention_grad = (
        factor * grad_heads - attention * (factor * factor * factor) * mean_term
    ).astype(jnp.bfloat16)
    grad_scores = jnp.einsum(
        "shj,thj->hst", attention_grad, value_heads, preferred_element_type=jnp.float32
    )
    grad_scores = (grad_scores * causal).astype(jnp.bfloat16)
    local_grad = jnp.einsum(
        "chi,chj->hij", query_heads, attention_grad, preferred_element_type=jnp.float32
    )
    suffix_state = prefix(local_grad, "seq", add_states, jnp.zeros_like(local_grad))
    suffix_rounded = suffix_state.astype(jnp.bfloat16)
    query_grad = jnp.einsum(
        "shj,hij->shi", attention_grad, prefix_rounded, preferred_element_type=jnp.float32
    )
    query_grad = query_grad + jnp.einsum(
        "hst,thi->shi", grad_scores, key_heads, preferred_element_type=jnp.float32
    )
    key_grad = jnp.einsum(
        "thj,hij->thi", value_heads, suffix_rounded, preferred_element_type=jnp.float32
    )
    key_grad = key_grad + jnp.einsum(
        "hst,shi->thi", grad_scores, query_heads, preferred_element_type=jnp.float32
    )
    value_grad = jnp.einsum(
        "thi,hij->thj", key_heads, suffix_rounded, preferred_element_type=jnp.float32
    )
    value_grad = value_grad + jnp.einsum(
        "hst,shj->thj", block_scores, attention_grad, preferred_element_type=jnp.float32
    )

    def finish(tensor):
        return tensor.astype(jnp.bfloat16).reshape(1, positions_count, features)

    return (layer_output, finish(query_grad), finish(key_grad), finish(value_grad))


MESH = pl.DeviceIdType.MESH
F32, BF16 = jnp.float32, jnp.bfloat16
PIECES = ((0, 2), (2, 2), (4, 2), (6, 1), (7, 1))
GROUPS = 4
EARLY = 6
LATE = 3
ORDER = (0, 1, 3, 4, 2)


def dot(a, b, ca, cb):
    return lax.dot_general(a, b, (((ca,), (cb,)), ((), ())), preferred_element_type=F32)


def body(nz, head_count, rows, wd, *refs):
    (q_in, k_in, v_in, w, cot, out, qg, kg, vg, wg, cotg, lst, pin, pout, scores, att, normg, acc, ngs, ngr,
     osend, orecv, oacc, ofin, ag, kloc, vloc, near, far, sout,
     q, k, v, in_sem, own_sem, w_s, w_r, c_s, c_r, r_s, r_r, p_s, p_r, a_s, a_r, b_s, b_r, n_s, n_r, g_s, g_r, o_s, o_r, f_s, f_r) = refs
    z, x = lax.axis_index("seq"), lax.axis_index("dp")
    y, s = lax.axis_index("groups"), lax.axis_index("sub")
    half, hb, feat = wd // 2, nz // 2, head_count * HS
    per = head_count // GROUPS
    last = nz - 1
    peers = (3, 1, 2)

    def place(j):
        return lax.rem(x + (j & 1), 2), lax.rem(y + (j >> 1), 2)

    def to_peer(j):
        xj, yj = place(j)
        return {"dp": xj, "groups": yj}

    def remote(src, dst, send, recv, device):
        return pltpu.make_async_remote_copy(
            src_ref=src, dst_ref=dst, send_sem=send, recv_sem=recv, device_id=device, device_id_type=MESH)

    other = {"sub": 1 - s}

    loads = [pltpu.make_async_copy(a, b, in_sem.at[i]) for i, (a, b) in enumerate(((k_in, k), (v_in, v), (q_in, q)))]
    barrier = pltpu.get_barrier_semaphore()
    for j in peers:
        pl.semaphore_signal(barrier, inc=1, device_id=to_peer(j), device_id_type=MESH)
    for d in range(1, nz):
        pl.semaphore_signal(barrier, inc=1, device_id={"seq": lax.rem(z + d, nz)}, device_id_type=MESH)
    pl.semaphore_signal(barrier, inc=1, device_id=other, device_id_type=MESH)
    for load in loads:
        load.start()
    pl.semaphore_wait(barrier, nz + 3)

    mine = w.at[:, pl.ds(pl.multiple_of(y * half, 128), half)]
    sent = {zz: [] for zz in range(nz)}

    def span(c):
        first, count = PIECES[c]
        return slice(first * HS, (first + count) * HS)

    def w_copy(zz, block, c, dz):
        src = mine if block == zz else wg.at[block]
        return remote(src.at[span(c)], wg.at[block, span(c)], w_s.at[(dz + 1) // 2, block, c], w_r.at[block, c], {"seq": zz + dz})

    def prefix_copy(zz, g):
        part = pl.ds(g * per, per)
        return remote(pout.at[part], pin.at[part], p_s.at[g], p_r.at[g], {"seq": zz + 1})

    def heads_of(c):
        first, count = PIECES[c]
        return pl.ds(first, count)

    def near_copy(zz, c):
        return remote(sout.at[heads_of(c)], near.at[heads_of(c)], a_s.at[c], a_r.at[c], {"seq": zz - 1})

    def far_to(c):
        return range(0 if c >= LATE else 1, last)

    def far_copy(to, c):
        return remote(sout.at[heads_of(c)], far.at[heads_of(c)], b_s.at[to, c], b_r.at[c], {"seq": to})

    def stage(table):
        for zz, ops in table.items():
            @pl.when(z == zz)
            def _():
                for op in ops:
                    if op[0] == "w":
                        copy = w_copy(zz, *op[1:])
                        if op[1] != zz:
                            w_copy(zz, op[1], op[2], op[3]).wait_recv()
                        copy.start()
                        sent[zz].append((w_copy, op[1:]))
                    elif op[0] == "p":
                        g = op[1]
                        part = slice(g * per, (g + 1) * per)
                        copy = prefix_copy(min(zz, last - 1), g)
                        if zz > 0:
                            copy.wait_recv()
                        if zz == 0:
                            pout[part] = lst[part].astype(BF16)
                            pin[part] = jnp.zeros((per, HS, HS), BF16)
                        elif zz < last:
                            pout[part] = (pin[part].astype(F32) + lst[part]).astype(BF16)
                        if zz < last:
                            copy.start()
                            sent[zz].append((prefix_copy, (g,)))

    def own(c, *ways):
        return [("w", None, c, way) for way in ways]

    def table(**rows_of):
        made = {}
        for name, ops in rows_of.items():
            zz = int(name[1:])
            made[zz] = [tuple(zz if (i == 1 and part is None) else part for i, part in enumerate(op)) for op in ops]
        return made

    stage(table(
        z0=own(0, 1),
        z1=own(0, 1, -1) + own(1, 1, -1),
        z2=own(0, 1, -1) + own(1, 1, -1),
        z3=[op for c in range(len(PIECES)) for op in own(c, -1)],
    ))
    own_w = pltpu.make_async_copy(mine, wg.at[z], own_sem.at[nz])
    own_w.start()

    share = pl.ds(pl.multiple_of(s * (rows // 2), rows // 2), rows // 2)

    def cot_piece(j, b, which):
        xj, yj = place(j)
        return cot.at[0, which, pl.ds(pl.multiple_of((b * 2 + xj) * wd + yj * half, 128), half)]

    def cot_own(b):
        return pltpu.make_async_copy(cot_piece(0, b, slice(None)), cotg.at[b, 0], own_sem.at[b])

    def cot_copy(j, b):
        return remote(cot_piece(j, b, share), cotg.at[b, j, share], c_s.at[j, b], c_r.at[j, b], to_peer(j))

    def cot_across(j):
        return remote(cotg.at[:, j, share], cotg.at[:, j, share], r_s.at[j], r_r.at[j], other)

    for b in range(nz):
        cot_own(b).start()
        for j in peers:
            cot_copy(j, b).start()

    def col(h):
        return slice(h * HS, (h + 1) * HS)

    for load in loads:
        load.wait()
    for h in range(head_count):
        lst[h] = dot(k[0, :, col(h)], v[0, :, col(h)], 0, 0)
    stage(table(
        z0=[("p", g) for g in range(GROUPS)] + [op for c in range(1, len(PIECES)) for op in own(c, 1)],
    ))

    @pl.when(z >= 2)
    def _():
        near[...] = jnp.zeros(near.shape, BF16)

    @pl.when(z == last)
    def _():
        far[...] = jnp.zeros(far.shape, BF16)

    @pl.when(z == 0)
    def _():
        for c in range(LATE):
            part = heads_of(c)
            far[part] = jnp.zeros((PIECES[c][1], HS, HS), BF16)

    causal = (lax.broadcasted_iota(jnp.int32, (rows, rows), 1) <= lax.broadcasted_iota(jnp.int32, (rows, rows), 0))
    for h in range(head_count):
        product = dot(q[0, :, col(h)], k[0, :, col(h)], 1, 1)
        scores[h] = jnp.where(causal, product, 0.0).astype(BF16)
    for h in range(head_count):
        att[h] = dot(scores[h], v[0, :, col(h)], 1, 0)

    def normed_copy(j, g):
        part = slice(g * per * HS, (g + 1) * per * HS)
        return remote(normg.at[0, :, part], normg.at[j, :, part], n_s.at[j, g], n_r.at[j, g], to_peer(j))

    def grad_copy(j, c):
        return remote(ngs.at[j, :, span(c)], ngr.at[j, :, span(c)], g_s.at[j, c], g_r.at[j, c], to_peer(j))

    def attend(g):
        for h in range(g * per, (g + 1) * per):
            total = att[h] + dot(q[0, :, col(h)], pin[h], 1, 0)
            att[h] = total
            factor = lax.rsqrt(jnp.mean(total * total, axis=-1, keepdims=True) + 1e-05)
            normg[0, :, col(h)] = (total * factor).astype(BF16)
        for j in peers:
            normed_copy(j, g).start()

    def gradient(c):
        for zz in (0, last):
            @pl.when(z == zz)
            def _():
                for b in range(nz):
                    if b != zz:
                        w_copy(zz, b, c, 1 if zz == 0 else -1).wait_recv()
        part = span(c)
        total = dot(cotg[0].reshape(4 * rows, half), wg[0, part, :], 1, 1)
        for b in range(1, nz):
            total = total + dot(cotg[b].reshape(4 * rows, half), wg[b, part, :], 1, 1)
        acc[:, part] = total[:rows]
        for j in peers:
            ngs[j, :, part] = total[j * rows:(j + 1) * rows].astype(BF16)
            grad_copy(j, c).start()

    def turn(c):
        first, count = PIECES[c]
        ready = []
        for h in range(first, first + count):
            total = att[h]
            factor = lax.rsqrt(jnp.mean(total * total, axis=-1, keepdims=True) + 1e-05)
            ready.append((h, total, factor, total * (factor * factor * factor)))
        for j in peers:
            grad_copy(j, c).wait_recv()
        for h, total, factor, scaled in ready:
            grad = acc[:, col(h)]
            for j in peers:
                grad = grad + ngr[j, :, col(h)].astype(F32)
            mean_term = jnp.mean(total * grad, axis=-1, keepdims=True)
            turned = (factor * grad - scaled * mean_term).astype(BF16)
            ag[h] = turned
            lst[h] = dot(q[0, :, col(h)], turned, 0, 0)
            sout[h] = lst[h].astype(BF16)

        @pl.when(z == last)
        def _():
            for to in reversed(far_to(c)) if c < LATE else far_to(c):
                far_copy(to, c).start()

        @pl.when(z == 2)
        def _():
            near_copy(2, c).start()

    def finish(c):
        first, count = PIECES[c]
        for h in range(first, first + count):
            turned = ag[h]
            grad_scores = jnp.where(causal, dot(turned, v[0, :, col(h)], 1, 1), 0.0).astype(BF16)
            qg[0, :, col(h)] = (dot(turned, pin[h], 1, 1) + dot(grad_scores, k[0, :, col(h)], 1, 0)).astype(BF16)
            kloc[h] = dot(grad_scores, q[0, :, col(h)], 0, 0)
            vloc[h] = dot(scores[h], turned, 0, 0)

    def up(block, c):
        return ("w", block, c, 1)

    def down(block, c):
        return ("w", block, c, -1)

    stage(table(
        z1=[up(0, 0), down(2, 0)],
        z2=[up(1, 0), down(3, 0)],
    ))
    for g in range(GROUPS):
        stage(table(
            z1=[("p", g)] + ([down(2, 1)] if g == 0 else [down(3, 0)] if g == GROUPS - 1 else []),
            z2=([up(1, 1), down(3, 1), up(0, 0)] + own(2, -1) if g == 0 else []) + [("p", g)],
            z3=[("p", g)],
        ))
        attend(g)
        if g == 0:
            for j in peers:
                for b in range(nz):
                    cot_copy(j, b).wait_recv()
                cot_across(j).start()
    stage(table(
        z1=[up(0, 1), down(3, 1)] + own(2, 1, -1),
        z2=[down(3, 2)] + own(3, -1) + [up(0, 1)] + own(2, 1),
    ))
    own_w.wait()
    for b in range(nz):
        cot_own(b).wait()
    for j in peers:
        cot_across(j).wait_recv()
    gradient(0)
    stage(table(
        z1=[up(0, 2), down(2, 2), down(3, 2)] + own(3, 1, -1),
        z2=[down(3, 3), up(1, 2), up(0, 2)] + own(3, 1),
    ))
    gradient(1)
    stage(table(
        z1=[up(0, 3), down(2, 3), down(3, 3)] + own(4, 1, -1) + [up(0, 4), down(2, 4), down(3, 4)],
        z2=own(4, -1) + [down(3, 4), up(1, 3), up(0, 3)] + own(4, 1) + [up(1, 4), up(0, 4)],
    ))
    gradient(2)
    turn(0)
    for j in peers:
        for g in range(GROUPS):
            normed_copy(j, g).wait_recv()
    deep = EARLY * HS

    @pl.loop(0, nz)
    def _(b):
        left = normg[:, :, :deep].reshape(4 * rows, deep)
        oacc[b] = dot(left, wg[b, :deep], 1, 0).reshape(4, rows, half)

    finish(0)
    gradient(3)
    turn(1)
    finish(1)
    turn(2)
    finish(2)
    gradient(4)

    def sub_copy(i):
        return remote(osend.at[i], orecv.at[i], o_s.at[i], o_r.at[i], other)

    left = normg[:, :, deep:].reshape(4 * rows, feat - deep)
    for i in range(hb):
        there = (1 - s) * hb + i
        osend[i] = (oacc[there] + dot(left, wg[there, deep:], 1, 0).reshape(4, rows, half)).astype(BF16)
        sub_copy(i).start()
    for i in range(hb):
        here = s * hb + i
        oacc[here] = oacc[here] + dot(left, wg[here, deep:], 1, 0).reshape(4, rows, half)
    turn(3)

    def out_part(i, xj, yj):
        return out.at[0, :, pl.ds(pl.multiple_of((i * 2 + xj) * wd + yj * half, 128), half)]

    def out_copy(i, j):
        return remote(ofin.at[i, j], out_part(i, x, y), f_s.at[i, j], f_r.at[i, j], to_peer(j))

    for i in range(hb):
        sub_copy(i).wait_recv()
        ofin[i] = (oacc[s * hb + i] + orecv[i].astype(F32)).astype(BF16)
        for j in peers:
            out_copy(i, j).start()
        out_part(i, x, y)[...] = ofin[i, 0]

    turn(4)

    @pl.when(z == 1)
    def _():
        for c in ORDER:
            near_copy(1, c).wait_recv()
            part = heads_of(c)
            added = near[part].astype(F32) + lst[part]
            if c < LATE:
                far_copy(1, c).wait_recv()
                added = added + far[part].astype(F32)
            sout[part] = added.astype(BF16)
            near_copy(1, c).start()

    finish(3)
    finish(4)
    for zz in range(nz):
        @pl.when(z == zz)
        def _():
            for make, where in sent[zz]:
                make(zz, *where).wait_send()
    for j in peers:
        for b in range(nz):
            cot_copy(j, b).wait_send()
        cot_across(j).wait_send()
        for g in range(GROUPS):
            normed_copy(j, g).wait_send()
        for c in range(len(PIECES)):
            grad_copy(j, c).wait_send()
    for i in range(hb):
        sub_copy(i).wait_send()

    for c in range(len(PIECES)):
        @pl.when(z == 0)
        def _():
            near_copy(1, c).wait_recv()

        if c < LATE:
            @pl.when(z == 2)
            def _():
                far_copy(2, c).wait_recv()
        else:
            @pl.when(z < last)
            def _():
                far_copy(0, c).wait_recv()
        first, count = PIECES[c]
        for h in range(first, first + count):
            carried = (near[h].astype(F32) + far[h].astype(F32)).astype(BF16)
            kg[0, :, col(h)] = (kloc[h] + dot(v[0, :, col(h)], carried, 1, 1)).astype(BF16)
            vg[0, :, col(h)] = (vloc[h] + dot(k[0, :, col(h)], carried, 1, 0)).astype(BF16)

    for i in range(hb):
        for j in peers:
            out_copy(i, j).wait_recv()

    for zz in range(nz):
        @pl.when(z == zz)
        def _():
            for c in range(len(PIECES)):
                if zz == last:
                    for to in far_to(c):
                        far_copy(to, c).wait_send()
                elif zz > 0:
                    near_copy(zz, c).wait_send()
    for j in peers:
        for i in range(hb):
            out_copy(i, j).wait_send()


def hand_over(*refs):
    copies = [pltpu.make_async_copy(refs[i], refs[4 + i], refs[8].at[i]) for i in range(4)]
    for copy in copies:
        copy.start()
    for copy in copies:
        copy.wait()


def fused(nz, queries, key_vectors, value_vectors, out_weight, out_cotangent):
    rows, feat = queries.shape[1:]
    wd = out_weight.shape[1]
    heads, half, hb, pieces = feat // HS, wd // 2, nz // 2, len(PIECES)
    vmem, dma = pltpu.VMEM, pltpu.SemaphoreType.DMA
    states = (heads, HS, HS)
    inside = pl.BlockSpec(memory_space=pltpu.VMEM)
    outside = pl.BlockSpec(memory_space=pltpu.HBM)
    grads = pltpu.VMEM((1, rows, feat), BF16)
    outs = pl.pallas_call(
        functools.partial(body, nz, heads, rows, wd),
        out_shape=(pltpu.VMEM((1, rows, nz * wd), BF16), grads, grads, grads),
        in_specs=[outside] * 5,
        out_specs=(inside,) * 4,
        scratch_shapes=[
            vmem((nz, feat, half), BF16), vmem((nz, 4, rows, half), BF16),
            vmem(states, F32), vmem(states, BF16), vmem(states, BF16),
            vmem((heads, rows, rows), BF16), vmem((heads, rows, HS), F32),
            vmem((4, rows, feat), BF16), vmem((rows, feat), F32),
            vmem((4, rows, feat), BF16), vmem((4, rows, feat), BF16),
            vmem((hb, 4, rows, half), BF16), vmem((hb, 4, rows, half), BF16),
            vmem((nz, 4, rows, half), F32), vmem((hb, 4, rows, half), BF16),
            vmem((heads, rows, HS), BF16), vmem((heads, rows, HS), F32), vmem((heads, rows, HS), F32),
            vmem(states, BF16), vmem(states, BF16), vmem(states, BF16),
            vmem((1, rows, feat), BF16), vmem((1, rows, feat), BF16), vmem((1, rows, feat), BF16), dma((3,)),
            dma((nz + 1,)), dma((2, nz, pieces)), dma((nz, pieces)),
            dma((4, nz)), dma((4, nz)), dma((4,)), dma((4,)), dma((GROUPS,)), dma((GROUPS,)),
            dma((pieces,)), dma((pieces,)), dma((nz, pieces)), dma((pieces,)),
            dma((4, GROUPS)), dma((4, GROUPS)), dma((4, pieces)), dma((4, pieces)),
            dma((hb,)), dma((hb,)), dma((hb, 4)), dma((hb, 4)),
        ],
        compiler_params=pltpu.CompilerParams(
            collective_id=0, has_side_effects=True, vmem_limit_bytes=60 * 1024 * 1024),
    )(queries, key_vectors, value_vectors, out_weight, out_cotangent)
    grads = jax.ShapeDtypeStruct((1, rows, feat), BF16)
    return tuple(pl.pallas_call(
        hand_over,
        out_shape=(jax.ShapeDtypeStruct((1, rows, nz * wd), BF16), grads, grads, grads),
        in_specs=[pl.BlockSpec(memory_space=pltpu.VMEM)] * 4,
        out_specs=(outside,) * 4,
        scratch_shapes=[dma((4,))],
    )(*(pltpu.with_memory_space_constraint(o, pltpu.VMEM) for o in outs)))


def solution(mesh):
    placed = (
        P(("groups", "dp"), "seq", "sub"),
        P(("groups", "dp"), "seq", "sub"),
        P(("groups", "dp"), "seq", "sub"),
        P("sub", ("seq", "dp")),
        P(("groups", "dp"), "seq", None),
    )
    shape = dict(mesh.shape)
    count = shape["seq"]

    def part(queries, key_vectors, value_vectors, out_weight, out_cotangent):
        args = (queries, key_vectors, value_vectors, out_weight, out_cotangent)
        fits = shape["groups"] == shape["dp"] == shape["sub"] == 2 and count == 4
        if fits and queries.shape[2] == 8 * HS and out_weight.shape[1] % 256 == 0:
            return fused(count, *args)
        return local(*args)

    return jax.shard_map(
        part,
        mesh=mesh,
        in_specs=placed,
        out_specs=(
            P(("groups", "dp"), "seq", "sub"),
            P(("groups", "dp"), "seq", "sub"),
            P(("groups", "dp"), "seq", "sub"),
            P(("groups", "dp"), "seq", "sub"),
        ),
        check_vma=False,
    )
```
